32 devices in a mesh: days: 2 (over x), chan: 16 (over z, y, core).
Axes of the slice: x: 2, y: 2, z: 4, core: 2. Of those that a mesh axis runs over, the one named last changes fastest.
Arguments:
- spectra: bfloat16 [8, 512, 2048], P('days', None, 'chan'), may hold values from -6 to 6
- sources: int32 [2], replicated, may hold values from 0 to 2047
- offsets: int32 [2048], P('chan'), may hold values from 0 to 4095
Outputs:
- slant: float32 [128, 2, 2, 256], P('chan')
The draws below stay inside these ranges and needn't reach their ends.
All inputs are finite; a program needn't handle non-finite values.
Results may differ from the reference program's by a relative error of at most 0.0055.
Values may be sent and summed in bfloat16 or wider, within the bound.
A program may use at most 64 MiB of HBM per device.

```python
import math
import jax
import jax.numpy as jnp
from jax import lax

BINS = 256
LAGS = 512
NSLOW = 128
NSRC = 2
CHANNELS = 2048
WINDOWS = 8


def touch_ends(array, key, low, top_value):
    shape = array.shape
    place = [jax.random.randint(jax.random.fold_in(key, axis), (), 0, shape[axis]) for axis in range(len(shape))]
    array = array.at[tuple(place)].set(low)
    longest = shape.index(max(shape))
    place[longest] = (place[longest] + 1) % shape[longest]
    return array.at[tuple(place)].set(top_value)


def block_levels(own_key, dims, shards, smallest, largest):
    level, own = 1.0, jax.random.fold_in(own_key, 6)
    for position, shards_of in shards:
        steps = jnp.exp(jax.random.uniform(jax.random.fold_in(own, position), (shards_of,), jnp.float32, smallest / len(shards), largest / len(shards)))
        level = level * jnp.repeat(steps, dims[position] // shards_of).reshape([-1 if axis == position else 1 for axis in range(len(dims))])
    return level


def noise(own_key, shape, spread, reach, cuts=(), kind=jnp.bfloat16):
    loudness = block_levels(own_key, shape, cuts, -0.22, 0.18) if cuts else 1.0
    result = jax.random.normal(own_key, shape, jnp.float32) * spread * loudness
    return jnp.minimum(jnp.maximum(result, -reach), reach).astype(kind)


def setup_inputs(seed: int = 0) -> dict:
    key_of = jax.random.split(jax.random.key(seed), 4)
    spectra = noise(key_of[0], (WINDOWS, 2 * BINS, CHANNELS), 1.0, 6.0, ((0, 2), (2, 16)))
    sources = jax.random.randint(key_of[1], (NSRC,), 0, CHANNELS).astype(jnp.int32)
    offsets = touch_ends(jax.random.randint(key_of[2], (CHANNELS,), 0, 4096), jax.random.fold_in(key_of[2], 1), 0, 4095).astype(jnp.int32)
    return {"spectra": spectra, "sources": sources, "offsets": offsets}


def angles(left_index, right_index, period):
    return (left_index * right_index % period).astype(jnp.float32) * (2.0 * math.pi / period)

def inverse_table(bins):
    lag_total = 2 * bins
    theta = angles(jnp.arange(lag_total, dtype=jnp.int32)[:, None], jnp.arange(bins, dtype=jnp.int32)[None, :], lag_total)
    cosine = jnp.cos(theta)
    sine = jnp.sin(theta)
    upper = jnp.concatenate([cosine, -sine], 1)
    lower = jnp.concatenate([sine, cosine], 1)
    return (jnp.concatenate([upper, lower], 0) / math.sqrt(bins)).astype(jnp.bfloat16)

def forward_table(bins, lag_first, lag_count):
    lag_total = 2 * bins
    theta = angles(jnp.arange(bins, dtype=jnp.int32)[:, None], lag_first + jnp.arange(lag_count, dtype=jnp.int32)[None, :], lag_total)
    return jnp.concatenate([jnp.cos(theta), -jnp.sin(theta)], 0) / math.sqrt(lag_total)

def slant_block(spec_re, spec_im, slowness, offsets, bins):
    freq = jnp.arange(bins, dtype=jnp.int32)
    phase = freq[None, :, None] * slowness[:, None, None] % 4096 * offsets[None, None, :] % 4096
    theta = phase.astype(jnp.float32) * (2.0 * math.pi / 4096)
    cosine = jnp.cos(theta)
    sine = jnp.sin(theta)
    highest = lax.Precision.HIGHEST
    real_part = jnp.einsum('sfc,kfc->ksf', spec_re, cosine, precision=highest) - jnp.einsum('sfc,kfc->ksf', spec_im, sine, precision=highest)
    imag_part = jnp.einsum('sfc,kfc->ksf', spec_re, sine, precision=highest) + jnp.einsum('sfc,kfc->ksf', spec_im, cosine, precision=highest)
    return jnp.stack([real_part, imag_part], 2)

def reference(spectra, sources, offsets):
    inverse = inverse_table(BINS).astype(jnp.float32)
    highest = lax.Precision.HIGHEST

    def one_window(totals, window):
        source_part = window[:, sources].T.astype(jnp.float32)
        channel_part = window.astype(jnp.float32)
        real_s = source_part[:, :BINS, None]
        imag_s = source_part[:, BINS:, None]
        real_x = channel_part[None, :BINS]
        imag_x = channel_part[None, BINS:]
        product = jnp.concatenate([real_s * real_x + imag_s * imag_x, real_s * imag_x - imag_s * real_x], 1)
        rounded = lax.optimization_barrier(product.astype(jnp.bfloat16)).astype(jnp.float32)
        analytic = jnp.einsum('lk,skc->slc', inverse, rounded, precision=highest)
        correlation = analytic[:, :LAGS]
        hilbert = analytic[:, LAGS:]
        magnitude = jnp.maximum(jnp.sqrt(correlation * correlation + hilbert * hilbert), 0.5)
        return ((totals[0] + correlation, totals[1] + correlation / magnitude, totals[2] + hilbert / magnitude), None)
    empty = jnp.zeros((NSRC, LAGS, CHANNELS), jnp.float32)
    (linear, phase_re, phase_im), _ = lax.scan(one_window, (empty, empty, empty), spectra)
    weighted = linear / WINDOWS * ((phase_re * phase_re + phase_im * phase_im) / (WINDOWS * WINDOWS))
    forward = forward_table(BINS, 0, LAGS)
    spectrum = jnp.einsum('kt,stc->skc', forward, weighted, precision=highest)
    spec_re = spectrum[:, :BINS]
    spec_im = spectrum[:, BINS:]
    scaling = WINDOWS ** 1.5 / math.sqrt(CHANNELS)
    group_size = math.gcd(NSLOW, 8)
    groups = jnp.arange(NSLOW, dtype=jnp.int32).reshape(NSLOW // group_size, group_size)

    def one_group(slowness):
        return slant_block(spec_re, spec_im, slowness, offsets, BINS)
    pieces = lax.map(one_group, groups)
    return pieces.reshape(NSLOW, NSRC, 2, BINS) * scaling
```

```python
import functools
import math

import jax
import jax.numpy as jnp
import numpy as np
from jax import lax
from jax.experimental import pallas as pl
from jax.experimental.pallas import tpu as pltpu
from jax.sharding import PartitionSpec as P

NSLOW = 128
NSRC = 2
PERIOD = 4096
MIRROR = NSLOW // 2
TILE = 8
LANES = 128
NEAR = 4


def tables(bins):
    lag_total = 2 * bins
    lag = np.arange(lag_total)[:, None]
    freq = np.arange(bins)[None, :]
    theta = (lag * freq % lag_total) * (2.0 * math.pi / lag_total)
    cosine, sine = np.cos(theta), np.sin(theta)
    inverse = np.concatenate(
        [np.concatenate([cosine, -sine], 1), np.concatenate([sine, cosine], 1)], 0
    ) / math.sqrt(bins)
    block = LANES // (2 * NSRC)
    parts = np.stack([cosine, -sine], 1).reshape(lag_total, 2, bins // block, block).transpose(0, 2, 1, 3)
    forward = np.repeat(parts[:, :, :, None], NSRC, 3).reshape(lag_total, -1) / math.sqrt(lag_total)
    return (
        inverse.astype(np.float32).astype(jnp.bfloat16),
        forward.astype(np.float32).astype(jnp.bfloat16),
    )


def cos_sin(steps, period):
    quarter = period // 4
    place = steps & (period - 1)
    quadrant = (place + quarter // 2) // quarter
    x = (place - quadrant * quarter).astype(jnp.float32) * (2.0 * math.pi / period)
    y = x * x
    sine = x * (1.0 + y * (-1.0 / 6 + y * (1.0 / 120 - y * (1.0 / 5040))))
    cosine = 1.0 + y * (-0.5 + y * (1.0 / 24 + y * (-1.0 / 720 + y * (1.0 / 40320))))
    odd = (quadrant & 1) == 1
    first = jnp.where(odd, sine, cosine)
    second = jnp.where(odd, cosine, sine)
    first = jnp.where(((quadrant + 1) & 2) == 2, -first, first)
    second = jnp.where((quadrant & 2) == 2, -second, second)
    return first, second


def exchange(source, target, send_sem, recv_sem, day, chan):
    return pltpu.make_async_remote_copy(
        src_ref=source,
        dst_ref=target,
        send_sem=send_sem,
        recv_sem=recv_sem,
        device_id={"days": day, "chan": chan},
        device_id_type=pl.DeviceIdType.MESH,
    )


def pack_halves(spectra_ref, kept, sent, day):
    count, depth, width = spectra_ref.shape
    half = width // 2
    left = lax.broadcasted_iota(jnp.int32, (depth, width), 1) < half
    upper = jnp.full((depth, width), day, jnp.int32) == 1
    for pair in range(count // 2):
        first = spectra_ref[2 * pair].astype(jnp.float32)
        second = spectra_ref[2 * pair + 1].astype(jnp.float32)
        lows = jnp.where(left, first, pltpu.roll(second, half, 1))
        highs = jnp.where(left, pltpu.roll(first, half, 1), second)
        kept[pair] = jnp.where(upper, highs, lows).astype(jnp.bfloat16)
        sent[pair] = jnp.where(upper, lows, highs).astype(jnp.bfloat16)


def source_columns(spectra_ref, sources_ref, chan):
    count, depth, width = spectra_ref.shape
    shape = (count * NSRC, width)
    row = lax.broadcasted_iota(jnp.int32, shape, 0)
    channel = lax.broadcasted_iota(jnp.int32, shape, 1) + chan * width
    wanted = jnp.zeros(shape, jnp.int32)
    for s in range(NSRC):
        wanted = jnp.where(row % NSRC == s, sources_ref[s], wanted)
    total = 0.0
    for w in range(count):
        pick = ((channel == wanted) & (row // NSRC == w)).astype(jnp.float32).astype(jnp.bfloat16)
        total = total + lax.dot_general(
            pick, spectra_ref[w], (((1,), (1,)), ((), ())), preferred_element_type=jnp.float32
        )
    return total.astype(jnp.bfloat16)


def correlate(x_ref, source_rows, inverse_ref, analytic, first_slot):
    pairs, depth, width = x_ref.shape
    bins, half = depth // 2, width // 2
    wide = NSRC * width
    shape = (source_rows.shape[0], wide)
    rows = lax.broadcasted_iota(jnp.int32, shape, 0)
    lane = lax.broadcasted_iota(jnp.int32, shape, 1)
    for pair in range(pairs):
        wanted = (2 * pair + lane % width // half) * NSRC + lane // width
        pick = (rows == wanted).astype(jnp.float32).astype(jnp.bfloat16)
        source = lax.dot_general(
            source_rows, pick, (((0,), (0,)), ((), ())), preferred_element_type=jnp.float32
        )
        channel = x_ref[pair].astype(jnp.float32)
        channel = jnp.concatenate([channel] * NSRC, 1)
        real_s, imag_s = source[:bins], source[bins:]
        real_x, imag_x = channel[:bins], channel[bins:]
        product = jnp.concatenate(
            [real_s * real_x + imag_s * imag_x, real_s * imag_x - imag_s * real_x], 0
        ).astype(jnp.bfloat16)
        analytic[first_slot + pair] = jnp.dot(
            inverse_ref[...], product, preferred_element_type=jnp.float32
        )


def stack_sums(analytic, slots, start, block, lags, totals):
    linear, phase_re, phase_im = totals
    for slot in slots:
        corr = analytic[slot, pl.ds(start, block)]
        hilb = analytic[slot, pl.ds(lags + start, block)]
        over = jnp.minimum(lax.rsqrt(corr * corr + hilb * hilb), 2.0)
        linear = linear + corr
        phase_re = phase_re + corr * over
        phase_im = phase_im + hilb * over
    return linear, phase_re, phase_im


def first_stacks(analytic, slots, held):
    lags = analytic.shape[1] // 2
    block = 16

    def stack(step, carry):
        start = pl.multiple_of(step * block, block)
        totals = stack_sums(analytic, slots, start, block, lags, (0.0, 0.0, 0.0))
        for index, total in enumerate(totals):
            held[index, pl.ds(start, block)] = total
        return carry

    lax.fori_loop(0, lags // block, stack, 0, unroll=4)


def last_stacks(analytic, slots, held, weighted, factor):
    lags, width = analytic.shape[1] // 2, analytic.shape[2] // NSRC
    half = width // 2
    block = 16

    def stack(step, carry):
        start = pl.multiple_of(step * block, block)
        totals = tuple(held[index, pl.ds(start, block)] for index in range(3))
        totals = stack_sums(analytic, slots, start, block, lags, totals)

        def fold(value):
            parts = []
            for s in range(NSRC):
                part = value[:, s * width : (s + 1) * width]
                parts.append(part + pltpu.roll(part, half, 1))
            side = lax.broadcasted_iota(jnp.int32, (block, width), 1) < half
            return jnp.where(side, parts[0], parts[1])

        linear, phase_re, phase_im = (fold(total) for total in totals)
        result = linear * (phase_re * phase_re + phase_im * phase_im) * factor
        weighted[pl.ds(start, block)] = result.astype(jnp.bfloat16)
        return carry

    lax.fori_loop(0, lags // block, stack, 0, unroll=4)


def own_offsets(offset_ref, half, day):
    row = jnp.broadcast_to(offset_ref[...].reshape(1, 2 * half), (TILE, 2 * half))
    lane = lax.broadcasted_iota(jnp.int32, row.shape, 1)
    return jnp.where(lane // half == day, row, pltpu.roll(row, half, 1))


def phase_table(offsets, phases, first, last, half):
    period = 2 * PERIOD
    per = LANES // half
    sub = lax.broadcasted_iota(jnp.int32, (TILE, LANES), 0)
    lane = lax.broadcasted_iota(jnp.int32, (TILE, LANES), 1)
    side = lane // half
    odd = (2 * sub + 1) * offsets

    def group(number, carry):
        base = number * TILE
        jumps_cos, jumps_sin = cos_sin(((base + sub) * per + side) * (offsets * (2 * TILE)), period)
        for member in range(TILE):
            freq = (base + member) * per + side
            cosine, sine = cos_sin(odd * freq, period)
            jump_cos = jnp.broadcast_to(jumps_cos[member : member + 1], (TILE, LANES))
            jump_sin = jnp.broadcast_to(jumps_sin[member : member + 1], (TILE, LANES))
            twice = 2.0 * jump_cos
            now = [cosine, sine]
            before = [cosine * jump_cos + sine * jump_sin, sine * jump_cos - cosine * jump_sin]
            rows = [[], []]
            for step in range(MIRROR // TILE):
                for piece in range(2):
                    rows[piece].append(now[piece])
                    later = twice * now[piece] - before[piece]
                    before[piece], now[piece] = now[piece], later
            for piece in range(2):
                for step in range(0, MIRROR // TILE, 2):
                    tile = jnp.concatenate(rows[piece][step : step + 2], 0).astype(jnp.bfloat16)
                    phases[base + member, pl.ds(piece * MIRROR + step * TILE, 2 * TILE)] = tile
        return carry

    lax.fori_loop(first // TILE, last // TILE, group, 0)


def centre_table(offsets, centre, half, bins):
    block = LANES // (2 * NSRC)
    column = jnp.broadcast_to(offsets[:1].astype(jnp.float32), (LANES, LANES)).T[:half].astype(jnp.int32)
    lane = lax.broadcasted_iota(jnp.int32, (half, LANES), 1)
    freq = lane % block

    def one(number, carry):
        cosine, sine = cos_sin((number * block + freq) * (column * (NSLOW - 1)), 2 * PERIOD)
        centre[number, 0] = cosine
        centre[number, 1] = jnp.where(lane < LANES // 2, -sine, sine)
        return carry

    lax.fori_loop(0, bins // block, one, 0)


def mask_table(masks):
    block = masks.shape[0]
    lane = lax.broadcasted_iota(jnp.int32, masks.shape[1:], 1) % block
    for f in range(block):
        masks[f] = (lane == f).astype(jnp.float32).astype(jnp.bfloat16)


def turned_spectra(weighted, forward_ref, centre, spectra_out, half):
    block = LANES // (2 * NSRC)
    result = lax.dot_general(
        weighted[...], forward_ref[...], (((0,), (0,)), ((), ())), preferred_element_type=jnp.float32
    )
    own = lax.broadcasted_iota(jnp.int32, (half, LANES), 1) // block % NSRC == 0
    for number in range(spectra_out.shape[0]):
        part = result[:, number * LANES : (number + 1) * LANES]
        part = jnp.where(own, part[:half], part[half:])
        turned = part * centre[number, 0] + pltpu.roll(part, LANES // 2, 1) * centre[number, 1]
        spectra_out[number] = turned.astype(jnp.bfloat16)


def slant(phases, turned, masks, spread, number, half):
    block = masks.shape[0]
    per = LANES // half
    value = turned[number]
    for f in range(block):
        for piece in range(0, half, 2 * TILE):
            spread[f * half + piece : f * half + piece + 2 * TILE] = value[piece : piece + 2 * TILE] * masks[f]
    count = block // per
    left = jnp.concatenate([phases[number * count + index] for index in range(count)], 1)
    result = jnp.dot(left, spread[...], preferred_element_type=jnp.float32)
    even, odd = result[:MIRROR], pltpu.roll(result[MIRROR:], LANES // 2, 1)
    odd = jnp.where(lax.broadcasted_iota(jnp.int32, odd.shape, 1) < LANES // 2, -odd, odd)
    return even - odd, even + odd


def kernel(
    windows, scaling, days, chans, spectra_hbm, sources_ref, offset_ref, inverse_hbm, forward_hbm, out_ref,
    kept, sent, got, column, columns_far, plane, columns_near, analytic, weighted, turned, centre, masks, spread, phases, held,
    spectra_ref, leaving, arriving, owned, landing, inverse_ref, forward_ref, table_sem,
    half_sem, far_sem, near_sem, leave_sem, own_sem,
):
    count, depth, width = spectra_ref.shape
    bins, half = depth // 2, width // 2
    far = chans // NEAR
    rows = NSLOW // chans
    day, chan = lax.axis_index("days"), lax.axis_index("chan")
    high, low = chan // NEAR, chan % NEAR
    table_copies = [
        pltpu.make_async_copy(inverse_hbm, inverse_ref, table_sem.at[0]),
        pltpu.make_async_copy(forward_hbm, forward_ref, table_sem.at[1]),
    ]
    near_peers = [
        (dd, dl, (day + dd) % days, (low + dl) % NEAR)
        for dd in range(days)
        for dl in range(NEAR)
        if dd or dl
    ]
    far_peers = [
        (dd, dh, (day + dd) % days, (high + dh) % far)
        for dd in range(days)
        for dh in range(far)
        if dd or dh
    ]
    barrier = pltpu.get_barrier_semaphore()
    greeted = 0
    for dd, dl, to_day, to_low in near_peers:
        pl.semaphore_signal(
            barrier, inc=1, device_id={"days": to_day, "chan": high * NEAR + to_low},
            device_id_type=pl.DeviceIdType.MESH,
        )
        greeted += 1
    for dd, dh, to_day, to_high in far_peers:
        if dh:
            pl.semaphore_signal(
                barrier, inc=1, device_id={"days": to_day, "chan": to_high * NEAR + low},
                device_id_type=pl.DeviceIdType.MESH,
            )
            greeted += 1
    spectra_copy = pltpu.make_async_copy(spectra_hbm, spectra_ref, table_sem.at[2])
    spectra_copy.start()
    for copy in table_copies:
        copy.start()
    spectra_copy.wait()
    column[...] = source_columns(spectra_ref, sources_ref, chan)
    pack_halves(spectra_ref, kept, sent, day)
    pl.semaphore_wait(barrier, greeted)

    far_copies = []
    for dd, dh, to_day, to_high in far_peers:
        if dd == 0:
            copy = exchange(
                column, columns_far.at[dh - 1], far_sem.at[0, dh - 1], far_sem.at[1, dh - 1],
                day, to_high * NEAR + low,
            )
            copy.start()
            far_copies.append(copy)
    half_copy = exchange(sent, got, half_sem.at[0], half_sem.at[1], (day + 1) % days, chan)
    half_copy.start()
    offsets = own_offsets(offset_ref, half, day)
    blocks = phases.shape[0]
    phase_table(offsets, phases, 0, blocks // 2, half)
    total = column[...].astype(jnp.float32)
    for index, copy in enumerate(far_copies):
        copy.wait_recv()
        total = total + columns_far[index].astype(jnp.float32)
    plane[...] = total.astype(jnp.bfloat16)
    near_copies = []
    for index, (dd, dl, to_day, to_low) in enumerate(near_peers):
        copy = exchange(
            plane, columns_near.at[index], near_sem.at[0, index], near_sem.at[1, index],
            to_day, high * NEAR + to_low,
        )
        copy.start()
        near_copies.append((dd, copy))
    phase_table(offsets, phases, blocks // 2, blocks, half)
    centre_table(offsets, centre, half, bins)
    mask_table(masks)

    def gather(wanted, value):
        for index, (dd, copy) in enumerate(near_copies):
            if dd == wanted:
                copy.wait_recv()
                value = value + columns_near[index].astype(jnp.float32)
        return value.astype(jnp.bfloat16)

    pairs = count // 2
    rows_own = gather(0, total)
    for copy in table_copies:
        copy.wait()
    correlate(kept, rows_own, inverse_ref, analytic, 0)
    first_stacks(analytic, range(pairs), held)
    rows_other = gather(1, 0.0)
    half_copy.wait_recv()
    correlate(got, rows_other, inverse_ref, analytic, pairs)
    others = range(pairs, 2 * pairs)
    last_stacks(analytic, others, held, weighted, scaling / windows**3)
    turned_spectra(weighted, forward_ref, centre, turned, half)

    wire = leaving.dtype
    blocks_own = turned.shape[0] // days
    leave_copies = []
    for turn in range(days):
        shift = days - 1 - turn
        target = (day + shift) % days
        for pair in range(blocks_own // 2):
            ends = [
                slant(phases, turned, masks, spread.at[turn % 2, at], target * blocks_own + 2 * pair + at, half)
                for at in range(2)
            ]
            for owner in range(chans):
                upper = owner * rows >= MIRROR
                first = owner * rows - MIRROR if upper else MIRROR - (owner + 1) * rows
                both = [end[upper][first : first + rows] for end in ends]
                leaving[target, owner % NEAR, owner // NEAR, pair] = jnp.concatenate(both, 0).astype(wire)
        for hi in range(far):
            for index, (dd, dl, to_day, to_low) in enumerate(near_peers):
                if dd == shift:
                    copy = exchange(
                        leaving.at[target, to_low, hi], arriving.at[hi, index],
                        leave_sem.at[0, hi, index], leave_sem.at[1, hi, index],
                        target, high * NEAR + to_low,
                    )
                    copy.start()
                    leave_copies.append((hi, copy))
    for hi in range(far):
        total = leaving[day, low, hi].astype(jnp.float32)
        index = 0
        for at, copy in leave_copies:
            if at == hi:
                copy.wait_recv()
        for index in range(len(near_peers)):
            total = total + arriving[hi, index].astype(jnp.float32)
        owned[hi] = total.astype(wire)
        step = (hi - high) % far
        for dd in range(days):
            def send(dd=dd, hi=hi, step=step):
                exchange(
                    owned.at[hi], landing.at[dd, step], own_sem.at[0, dd, step], own_sem.at[1, dd, step],
                    (day + dd) % days, hi * NEAR + low,
                ).start()

            if dd:
                send()
            else:
                pl.when(step != 0)(send)

    def landed(dd, dh):
        return exchange(
            owned.at[0], landing.at[dd, dh], own_sem.at[0, dd, dh], own_sem.at[1, dd, dh],
            (day + dd) % days, (high + dh) % far * NEAR + low,
        )

    block = LANES // (2 * NSRC)
    for dd in range(days):
        total = 0.0
        for dh in range(far):
            if dd or dh:
                landed(dd, dh).wait_recv()
                total = total + landing[dd, dh].astype(jnp.float32)
            else:
                total = owned[high].astype(jnp.float32)
        pieces = [total[pair, at * rows : (at + 1) * rows] for pair in range(blocks_own // 2) for at in range(2)]
        for part in range(blocks_own * block // LANES):
            some = pieces[part * LANES // block : (part + 1) * LANES // block]
            for s in range(NSRC):
                for p in range(2):
                    begin = (p * NSRC + s) * block
                    value = jnp.concatenate([piece[:, begin : begin + block] for piece in some], 1)
                    mirrored = jnp.concatenate([value[row : row + 1] for row in reversed(range(rows))], 0)
                    lower = jnp.full(value.shape, chan * rows, jnp.int32) < MIRROR
                    out_ref[s, p, (day + dd) % days, part] = jnp.where(lower, mirrored, value)
    half_copy.wait_send()
    for copy in far_copies:
        copy.wait_send()
    for dd, copy in near_copies:
        copy.wait_send()
    for hi, copy in leave_copies:
        copy.wait_send()
    for dd in range(days):
        for dh in range(far):
            if dd or dh:
                landed(dd, dh).wait_send()


def shards(spectra, sources, offsets):
    count, depth, width = spectra.shape
    bins, half = depth // 2, width // 2
    days, chans = lax.axis_size("days"), lax.axis_size("chan")
    windows = count * days
    inverse, forward = tables(bins)
    scaling = windows**1.5 / math.sqrt(width * chans)
    far, rows, pairs = chans // NEAR, NSLOW // chans, count // 2
    near_count = days * NEAR - 1
    wire = jnp.bfloat16 if rows % TILE == 0 else jnp.float32
    block = LANES // (2 * NSRC)
    blocks = bins // block
    chunk = (blocks // days // 2, 2 * rows, LANES)
    parts = bins // days // LANES
    vmem = pl.BlockSpec(memory_space=pltpu.VMEM)
    smem = pl.BlockSpec(memory_space=pltpu.SMEM)
    anywhere = pl.BlockSpec(memory_space=pl.ANY)
    bf16, f32 = jnp.bfloat16, jnp.float32
    dma = pltpu.SemaphoreType.DMA
    out = pl.pallas_call(
        functools.partial(kernel, windows, scaling, days, chans),
        out_shape=jax.ShapeDtypeStruct((NSRC, 2, days, parts, rows, LANES), f32),
        in_specs=[anywhere, smem, vmem, anywhere, anywhere],
        out_specs=vmem,
        scratch_shapes=[
            pltpu.VMEM((pairs, depth, width), bf16),
            pltpu.VMEM((pairs, depth, width), bf16),
            pltpu.VMEM((pairs, depth, width), bf16),
            pltpu.VMEM((count * NSRC, depth), bf16),
            pltpu.VMEM((far - 1, count * NSRC, depth), bf16),
            pltpu.VMEM((count * NSRC, depth), bf16),
            pltpu.VMEM((near_count, count * NSRC, depth), bf16),
            pltpu.VMEM((2 * pairs, 2 * depth, NSRC * width), f32),
            pltpu.VMEM((depth, width), bf16),
            pltpu.VMEM((blocks, half, LANES), bf16),
            pltpu.VMEM((blocks, 2, half, LANES), f32),
            pltpu.VMEM((block, 2 * TILE, LANES), bf16),
            pltpu.VMEM((2, 2, block * half, LANES), bf16),
            pltpu.VMEM((bins * half // LANES, NSLOW, LANES), bf16),
            pltpu.VMEM((3, depth, NSRC * width), f32),
            pltpu.VMEM((count, depth, width), bf16),
            pltpu.VMEM((days, NEAR, far) + chunk, wire),
            pltpu.VMEM((far, near_count) + chunk, wire),
            pltpu.VMEM((far,) + chunk, wire),
            pltpu.VMEM((days, far) + chunk, wire),
            pltpu.VMEM(inverse.shape, bf16),
            pltpu.VMEM(forward.shape, bf16),
            dma((3,)),
            dma((2,)),
            dma((2, far - 1)),
            dma((2, near_count)),
            dma((2, far, near_count)),
            dma((2, days, far)),
        ],
        compiler_params=pltpu.CompilerParams(
            collective_id=0, has_side_effects=True, vmem_limit_bytes=40 * 1024 * 1024
        ),
    )(spectra, sources, offsets, jnp.asarray(inverse), jnp.asarray(forward))
    return out.transpose(4, 0, 1, 2, 3, 5).reshape(rows, NSRC, 2, bins)


def solution(mesh):
    placed = (P("days", None, "chan"), P(), P("chan"))
    return jax.shard_map(
        shards, mesh=mesh, in_specs=placed, out_specs=P("chan", None, None, None), check_vma=False
    )
```

```python
import functools
import math

import jax
import jax.numpy as jnp
import numpy as np
from jax import lax
from jax.experimental import pallas as pl
from jax.experimental.pallas import tpu as pltpu
from jax.sharding import PartitionSpec as P

NSLOW = 128
NSRC = 2
PERIOD = 4096
MIRROR = NSLOW // 2
TILE = 8
LANES = 128
NEAR = 4


def tables(bins):
    lag_total = 2 * bins
    lag = np.arange(lag_total)[:, None]
    freq = np.arange(bins)[None, :]
    theta = (lag * freq % lag_total) * (2.0 * math.pi / lag_total)
    cosine, sine = np.cos(theta), np.sin(theta)
    inverse = np.concatenate(
        [np.concatenate([cosine, -sine], 1), np.concatenate([sine, cosine], 1)], 0
    ) / math.sqrt(bins)
    block = LANES // (2 * NSRC)
    parts = np.stack([cosine, -sine], 1).reshape(lag_total, 2, bins // block, block).transpose(0, 2, 1, 3)
    forward = np.repeat(parts[:, :, :, None], NSRC, 3).reshape(lag_total, -1) / math.sqrt(lag_total)
    return (
        inverse.astype(np.float32).astype(jnp.bfloat16),
        forward.astype(np.float32).astype(jnp.bfloat16),
    )


def cos_sin(steps, period):
    quarter = period // 4
    place = steps & (period - 1)
    quadrant = (place + quarter // 2) // quarter
    x = (place - quadrant * quarter).astype(jnp.float32) * (2.0 * math.pi / period)
    y = x * x
    sine = x * (1.0 + y * (-1.0 / 6 + y * (1.0 / 120 - y * (1.0 / 5040))))
    cosine = 1.0 + y * (-0.5 + y * (1.0 / 24 + y * (-1.0 / 720 + y * (1.0 / 40320))))
    odd = (quadrant & 1) == 1
    first = jnp.where(odd, sine, cosine)
    second = jnp.where(odd, cosine, sine)
    first = jnp.where(((quadrant + 1) & 2) == 2, -first, first)
    second = jnp.where((quadrant & 2) == 2, -second, second)
    return first, second


def exchange(source, target, send_sem, recv_sem, day, chan):
    return pltpu.make_async_remote_copy(
        src_ref=source,
        dst_ref=target,
        send_sem=send_sem,
        recv_sem=recv_sem,
        device_id={"days": day, "chan": chan},
        device_id_type=pl.DeviceIdType.MESH,
    )


def pack_halves(spectra_ref, kept, sent, day):
    count, depth, width = spectra_ref.shape
    half = width // 2
    left = lax.broadcasted_iota(jnp.int32, (depth, width), 1) < half
    upper = jnp.full((depth, width), day, jnp.int32) == 1
    for pair in range(count // 2):
        first = spectra_ref[2 * pair].astype(jnp.float32)
        second = spectra_ref[2 * pair + 1].astype(jnp.float32)
        lows = jnp.where(left, first, pltpu.roll(second, half, 1))
        highs = jnp.where(left, pltpu.roll(first, half, 1), second)
        kept[pair] = jnp.where(upper, highs, lows).astype(jnp.bfloat16)
        sent[pair] = jnp.where(upper, lows, highs).astype(jnp.bfloat16)


def source_columns(spectra_ref, sources_ref, chan):
    count, depth, width = spectra_ref.shape
    shape = (count * NSRC, width)
    row = lax.broadcasted_iota(jnp.int32, shape, 0)
    channel = lax.broadcasted_iota(jnp.int32, shape, 1) + chan * width
    wanted = jnp.zeros(shape, jnp.int32)
    for s in range(NSRC):
        wanted = jnp.where(row % NSRC == s, sources_ref[s], wanted)
    total = 0.0
    for w in range(count):
        pick = ((channel == wanted) & (row // NSRC == w)).astype(jnp.float32).astype(jnp.bfloat16)
        total = total + lax.dot_general(
            pick, spectra_ref[w], (((1,), (1,)), ((), ())), preferred_element_type=jnp.float32
        )
    return total.astype(jnp.bfloat16)


def correlate(x_ref, source_rows, inverse_ref, analytic, first_slot):
    pairs, depth, width = x_ref.shape
    bins, half = depth // 2, width // 2
    wide = NSRC * width
    shape = (source_rows.shape[0], wide)
    rows = lax.broadcasted_iota(jnp.int32, shape, 0)
    lane = lax.broadcasted_iota(jnp.int32, shape, 1)
    for pair in range(pairs):
        wanted = (2 * pair + lane % width // half) * NSRC + lane // width
        pick = (rows == wanted).astype(jnp.float32).astype(jnp.bfloat16)
        source = lax.dot_general(
            source_rows, pick, (((0,), (0,)), ((), ())), preferred_element_type=jnp.float32
        )
        channel = x_ref[pair].astype(jnp.float32)
        channel = jnp.concatenate([channel] * NSRC, 1)
        real_s, imag_s = source[:bins], source[bins:]
        real_x, imag_x = channel[:bins], channel[bins:]
        product = jnp.concatenate(
            [real_s * real_x + imag_s * imag_x, real_s * imag_x - imag_s * real_x], 0
        ).astype(jnp.bfloat16)
        analytic[first_slot + pair] = jnp.dot(
            inverse_ref[...], product, preferred_element_type=jnp.float32
        )


def stack_sums(analytic, slots, start, block, lags, totals):
    linear, phase_re, phase_im = totals
    for slot in slots:
        corr = analytic[slot, pl.ds(start, block)]
        hilb = analytic[slot, pl.ds(lags + start, block)]
        over = jnp.minimum(lax.rsqrt(corr * corr + hilb * hilb), 2.0)
        linear = linear + corr
        phase_re = phase_re + corr * over
        phase_im = phase_im + hilb * over
    return linear, phase_re, phase_im


def first_stacks(analytic, slots, held):
    lags = analytic.shape[1] // 2
    block = 16

    def stack(step, carry):
        start = pl.multiple_of(step * block, block)
        totals = stack_sums(analytic, slots, start, block, lags, (0.0, 0.0, 0.0))
        for index, total in enumerate(totals):
            held[index, pl.ds(start, block)] = total
        return carry

    lax.fori_loop(0, lags // block, stack, 0, unroll=4)


def last_stacks(analytic, slots, held, weighted, factor):
    lags, width = analytic.shape[1] // 2, analytic.shape[2] // NSRC
    half = width // 2
    block = 16

    def stack(step, carry):
        start = pl.multiple_of(step * block, block)
        totals = tuple(held[index, pl.ds(start, block)] for index in range(3))
        totals = stack_sums(analytic, slots, start, block, lags, totals)

        def fold(value):
            parts = []
            for s in range(NSRC):
                part = value[:, s * width : (s + 1) * width]
                parts.append(part + pltpu.roll(part, half, 1))
            side = lax.broadcasted_iota(jnp.int32, (block, width), 1) < half
            return jnp.where(side, parts[0], parts[1])

        linear, phase_re, phase_im = (fold(total) for total in totals)
        result = linear * (phase_re * phase_re + phase_im * phase_im) * factor
        weighted[pl.ds(start, block)] = result.astype(jnp.bfloat16)
        return carry

    lax.fori_loop(0, lags // block, stack, 0, unroll=4)


def own_offsets(offset_ref, half, day):
    row = jnp.broadcast_to(offset_ref[...].reshape(1, 2 * half), (TILE, 2 * half))
    lane = lax.broadcasted_iota(jnp.int32, row.shape, 1)
    return jnp.where(lane // half == day, row, pltpu.roll(row, half, 1))


def phase_table(offsets, phases, first, last, half):
    period = 2 * PERIOD
    per = LANES // half
    sub = lax.broadcasted_iota(jnp.int32, (TILE, LANES), 0)
    lane = lax.broadcasted_iota(jnp.int32, (TILE, LANES), 1)
    side = lane // half
    odd = (2 * sub + 1) * offsets

    def group(number, carry):
        base = number * TILE
        jumps_cos, jumps_sin = cos_sin(((base + sub) * per + side) * (offsets * (2 * TILE)), period)
        for member in range(TILE):
            freq = (base + member) * per + side
            cosine, sine = cos_sin(odd * freq, period)
            jump_cos = jnp.broadcast_to(jumps_cos[member : member + 1], (TILE, LANES))
            jump_sin = jnp.broadcast_to(jumps_sin[member : member + 1], (TILE, LANES))
            twice = 2.0 * jump_cos
            now = [cosine, sine]
            before = [cosine * jump_cos + sine * jump_sin, sine * jump_cos - cosine * jump_sin]
            rows = [[], []]
            for step in range(MIRROR // TILE):
                for piece in range(2):
                    rows[piece].append(now[piece])
                    later = twice * now[piece] - before[piece]
                    before[piece], now[piece] = now[piece], later
            for piece in range(2):
                for step in range(0, MIRROR // TILE, 2):
                    tile = jnp.concatenate(rows[piece][step : step + 2], 0).astype(jnp.bfloat16)
                    phases[base + member, pl.ds(piece * MIRROR + step * TILE, 2 * TILE)] = tile
        return carry

    lax.fori_loop(first // TILE, last // TILE, group, 0)


def centre_table(offsets, centre, half, bins):
    block = LANES // (2 * NSRC)
    column = jnp.broadcast_to(offsets[:1].astype(jnp.float32), (LANES, LANES)).T[:half].astype(jnp.int32)
    lane = lax.broadcasted_iota(jnp.int32, (half, LANES), 1)
    freq = lane % block

    def one(number, carry):
        cosine, sine = cos_sin((number * block + freq) * (column * (NSLOW - 1)), 2 * PERIOD)
        centre[number, 0] = cosine
        centre[number, 1] = jnp.where(lane < LANES // 2, -sine, sine)
        return carry

    lax.fori_loop(0, bins // block, one, 0)


def mask_table(masks):
    block = masks.shape[0]
    lane = lax.broadcasted_iota(jnp.int32, masks.shape[1:], 1) % block
    for f in range(block):
        masks[f] = (lane == f).astype(jnp.float32).astype(jnp.bfloat16)


def turned_spectra(weighted, forward_ref, centre, spectra_out, half):
    block = LANES // (2 * NSRC)
    result = lax.dot_general(
        weighted[...], forward_ref[...], (((0,), (0,)), ((), ())), preferred_element_type=jnp.float32
    )
    own = lax.broadcasted_iota(jnp.int32, (half, LANES), 1) // block % NSRC == 0
    for number in range(spectra_out.shape[0]):
        part = result[:, number * LANES : (number + 1) * LANES]
        part = jnp.where(own, part[:half], part[half:])
        turned = part * centre[number, 0] + pltpu.roll(part, LANES // 2, 1) * centre[number, 1]
        spectra_out[number] = turned.astype(jnp.bfloat16)


def slant(phases, turned, masks, spread, number, half):
    block = masks.shape[0]
    per = LANES // half
    value = turned[number]
    for f in range(block):
        for piece in range(0, half, 2 * TILE):
            spread[f * half + piece : f * half + piece + 2 * TILE] = value[piece : piece + 2 * TILE] * masks[f]
    count = block // per
    left = jnp.concatenate([phases[number * count + index] for index in range(count)], 1)
    result = jnp.dot(left, spread[...], preferred_element_type=jnp.float32)
    even, odd = result[:MIRROR], pltpu.roll(result[MIRROR:], LANES // 2, 1)
    odd = jnp.where(lax.broadcasted_iota(jnp.int32, odd.shape, 1) < LANES // 2, -odd, odd)
    return even - odd, even + odd


def kernel(
    windows, scaling, days, chans, spectra_hbm, sources_hbm, offset_hbm, inverse_hbm, forward_hbm, out_ref,
    kept, sent, got, column, columns_far, plane, columns_near, analytic, weighted, turned, centre, masks, spread, phases, held,
    spectra_ref, leaving, arriving, owned, landing, inverse_ref, forward_ref,
    sources_ref, offset_ref, table_sem,
    half_sem, far_sem, near_sem, leave_sem, own_sem,
):
    count, depth, width = spectra_ref.shape
    bins, half = depth // 2, width // 2
    far = chans // NEAR
    rows = NSLOW // chans
    day, chan = lax.axis_index("days"), lax.axis_index("chan")
    high, low = chan // NEAR, chan % NEAR
    table_copies = [
        pltpu.make_async_copy(inverse_hbm, inverse_ref, table_sem.at[0]),
        pltpu.make_async_copy(forward_hbm, forward_ref, table_sem.at[1]),
    ]
    near_peers = [
        (dd, dl, (day + dd) % days, (low + dl) % NEAR)
        for dd in range(days)
        for dl in range(NEAR)
        if dd or dl
    ]
    far_peers = [
        (dd, dh, (day + dd) % days, (high + dh) % far)
        for dd in range(days)
        for dh in range(far)
        if dd or dh
    ]
    barrier = pltpu.get_barrier_semaphore()
    greeted = 0
    for dd, dl, to_day, to_low in near_peers:
        pl.semaphore_signal(
            barrier, inc=1, device_id={"days": to_day, "chan": high * NEAR + to_low},
            device_id_type=pl.DeviceIdType.MESH,
        )
        greeted += 1
    for dd, dh, to_day, to_high in far_peers:
        if dh:
            pl.semaphore_signal(
                barrier, inc=1, device_id={"days": to_day, "chan": to_high * NEAR + low},
                device_id_type=pl.DeviceIdType.MESH,
            )
            greeted += 1
    spectra_copy = pltpu.make_async_copy(spectra_hbm, spectra_ref, table_sem.at[2])
    sources_copy = pltpu.make_async_copy(sources_hbm, sources_ref, table_sem.at[3])
    offset_copy = pltpu.make_async_copy(offset_hbm, offset_ref, table_sem.at[4])
    copies = [sources_copy, spectra_copy, offset_copy]
    for copy in copies + table_copies:
        copy.start()
    for copy in copies:
        copy.wait()
    column[...] = source_columns(spectra_ref, sources_ref, chan)
    pack_halves(spectra_ref, kept, sent, day)
    pl.semaphore_wait(barrier, greeted)

    far_copies = []
    for dd, dh, to_day, to_high in far_peers:
        if dd == 0:
            copy = exchange(
                column, columns_far.at[dh - 1], far_sem.at[0, dh - 1], far_sem.at[1, dh - 1],
                day, to_high * NEAR + low,
            )
            copy.start()
            far_copies.append(copy)
    half_copy = exchange(sent, got, half_sem.at[0], half_sem.at[1], (day + 1) % days, chan)
    half_copy.start()
    offsets = own_offsets(offset_ref, half, day)
    blocks = phases.shape[0]
    phase_table(offsets, phases, 0, blocks // 2, half)
    total = column[...].astype(jnp.float32)
    for index, copy in enumerate(far_copies):
        copy.wait_recv()
        total = total + columns_far[index].astype(jnp.float32)
    plane[...] = total.astype(jnp.bfloat16)
    near_copies = []
    for index, (dd, dl, to_day, to_low) in enumerate(near_peers):
        copy = exchange(
            plane, columns_near.at[index], near_sem.at[0, index], near_sem.at[1, index],
            to_day, high * NEAR + to_low,
        )
        copy.start()
        near_copies.append((dd, copy))
    phase_table(offsets, phases, blocks // 2, blocks, half)
    centre_table(offsets, centre, half, bins)
    mask_table(masks)

    def gather(wanted, value):
        for index, (dd, copy) in enumerate(near_copies):
            if dd == wanted:
                copy.wait_recv()
                value = value + columns_near[index].astype(jnp.float32)
        return value.astype(jnp.bfloat16)

    pairs = count // 2
    rows_own = gather(0, total)
    for copy in table_copies:
        copy.wait()
    correlate(kept, rows_own, inverse_ref, analytic, 0)
    first_stacks(analytic, range(pairs), held)
    rows_other = gather(1, 0.0)
    half_copy.wait_recv()
    correlate(got, rows_other, inverse_ref, analytic, pairs)
    others = range(pairs, 2 * pairs)
    last_stacks(analytic, others, held, weighted, scaling / windows**3)
    turned_spectra(weighted, forward_ref, centre, turned, half)

    wire = leaving.dtype
    blocks_own = turned.shape[0] // days
    leave_copies = []
    for turn in range(days):
        shift = days - 1 - turn
        target = (day + shift) % days
        for pair in range(blocks_own // 2):
            ends = [
                slant(phases, turned, masks, spread.at[turn % 2, at], target * blocks_own + 2 * pair + at, half)
                for at in range(2)
            ]
            for owner in range(chans):
                upper = owner * rows >= MIRROR
                first = owner * rows - MIRROR if upper else MIRROR - (owner + 1) * rows
                both = [end[upper][first : first + rows] for end in ends]
                leaving[target, owner % NEAR, owner // NEAR, pair] = jnp.concatenate(both, 0).astype(wire)
        for hi in range(far):
            for index, (dd, dl, to_day, to_low) in enumerate(near_peers):
                if dd == shift:
                    copy = exchange(
                        leaving.at[target, to_low, hi], arriving.at[hi, index],
                        leave_sem.at[0, hi, index], leave_sem.at[1, hi, index],
                        target, high * NEAR + to_low,
                    )
                    copy.start()
                    leave_copies.append((hi, copy))
    for hi in range(far):
        total = leaving[day, low, hi].astype(jnp.float32)
        index = 0
        for at, copy in leave_copies:
            if at == hi:
                copy.wait_recv()
        for index in range(len(near_peers)):
            total = total + arriving[hi, index].astype(jnp.float32)
        owned[hi] = total.astype(wire)
        step = (hi - high) % far
        for dd in range(days):
            def send(dd=dd, hi=hi, step=step):
                exchange(
                    owned.at[hi], landing.at[dd, step], own_sem.at[0, dd, step], own_sem.at[1, dd, step],
                    (day + dd) % days, hi * NEAR + low,
                ).start()

            if dd:
                send()
            else:
                pl.when(step != 0)(send)

    def landed(dd, dh):
        return exchange(
            owned.at[0], landing.at[dd, dh], own_sem.at[0, dd, dh], own_sem.at[1, dd, dh],
            (day + dd) % days, (high + dh) % far * NEAR + low,
        )

    block = LANES // (2 * NSRC)
    for dd in range(days):
        total = 0.0
        for dh in range(far):
            if dd or dh:
                landed(dd, dh).wait_recv()
                total = total + landing[dd, dh].astype(jnp.float32)
            else:
                total = owned[high].astype(jnp.float32)
        pieces = [total[pair, at * rows : (at + 1) * rows] for pair in range(blocks_own // 2) for at in range(2)]
        for part in range(blocks_own * block // LANES):
            some = pieces[part * LANES // block : (part + 1) * LANES // block]
            for s in range(NSRC):
                for p in range(2):
                    begin = (p * NSRC + s) * block
                    value = jnp.concatenate([piece[:, begin : begin + block] for piece in some], 1)
                    mirrored = jnp.concatenate([value[row : row + 1] for row in reversed(range(rows))], 0)
                    lower = jnp.full(value.shape, chan * rows, jnp.int32) < MIRROR
                    out_ref[s, p, (day + dd) % days, part] = jnp.where(lower, mirrored, value)
    half_copy.wait_send()
    for copy in far_copies:
        copy.wait_send()
    for dd, copy in near_copies:
        copy.wait_send()
    for hi, copy in leave_copies:
        copy.wait_send()
    for dd in range(days):
        for dh in range(far):
            if dd or dh:
                landed(dd, dh).wait_send()


def shards(spectra, sources, offsets):
    count, depth, width = spectra.shape
    bins, half = depth // 2, width // 2
    days, chans = lax.axis_size("days"), lax.axis_size("chan")
    windows = count * days
    inverse, forward = tables(bins)
    scaling = windows**1.5 / math.sqrt(width * chans)
    far, rows, pairs = chans // NEAR, NSLOW // chans, count // 2
    near_count = days * NEAR - 1
    wire = jnp.bfloat16 if rows % TILE == 0 else jnp.float32
    block = LANES // (2 * NSRC)
    blocks = bins // block
    chunk = (blocks // days // 2, 2 * rows, LANES)
    parts = bins // days // LANES
    vmem = pl.BlockSpec(memory_space=pltpu.VMEM)
    hbm = pl.BlockSpec(memory_space=pltpu.HBM)
    bf16, f32 = jnp.bfloat16, jnp.float32
    dma = pltpu.SemaphoreType.DMA
    out = pl.pallas_call(
        functools.partial(kernel, windows, scaling, days, chans),
        out_shape=pltpu.VMEM((NSRC, 2, days, parts, rows, LANES), f32),
        in_specs=[hbm] * 5,
        out_specs=vmem,
        scratch_shapes=[
            pltpu.VMEM((pairs, depth, width), bf16),
            pltpu.VMEM((pairs, depth, width), bf16),
            pltpu.VMEM((pairs, depth, width), bf16),
            pltpu.VMEM((count * NSRC, depth), bf16),
            pltpu.VMEM((far - 1, count * NSRC, depth), bf16),
            pltpu.VMEM((count * NSRC, depth), bf16),
            pltpu.VMEM((near_count, count * NSRC, depth), bf16),
            pltpu.VMEM((2 * pairs, 2 * depth, NSRC * width), f32),
            pltpu.VMEM((depth, width), bf16),
            pltpu.VMEM((blocks, half, LANES), bf16),
            pltpu.VMEM((blocks, 2, half, LANES), f32),
            pltpu.VMEM((block, 2 * TILE, LANES), bf16),
            pltpu.VMEM((2, 2, block * half, LANES), bf16),
            pltpu.VMEM((bins * half // LANES, NSLOW, LANES), bf16),
            pltpu.VMEM((3, depth, NSRC * width), f32),
            pltpu.VMEM((count, depth, width), bf16),
            pltpu.VMEM((days, NEAR, far) + chunk, wire),
            pltpu.VMEM((far, near_count) + chunk, wire),
            pltpu.VMEM((far,) + chunk, wire),
            pltpu.VMEM((days, far) + chunk, wire),
            pltpu.VMEM(inverse.shape, bf16),
            pltpu.VMEM(forward.shape, bf16),
            pltpu.SMEM(sources.shape, jnp.int32),
            pltpu.VMEM(offsets.shape, jnp.int32),
            dma((5,)),
            dma((2,)),
            dma((2, far - 1)),
            dma((2, near_count)),
            dma((2, far, near_count)),
            dma((2, days, far)),
        ],
        compiler_params=pltpu.CompilerParams(
            collective_id=0, has_side_effects=True, vmem_limit_bytes=56 * 1024 * 1024
        ),
    )(spectra, sources, offsets, jnp.asarray(inverse), jnp.asarray(forward))
    return out.transpose(4, 0, 1, 2, 3, 5).reshape(rows, NSRC, 2, bins)


def solution(mesh):
    placed = (P("days", None, "chan"), P(), P("chan"))
    return jax.shard_map(
        shards, mesh=mesh, in_specs=placed, out_specs=P("chan", None, None, None), check_vma=False
    )
```

```python
import functools
import math

import jax
import jax.numpy as jnp
import numpy as np
from jax import lax
from jax.experimental import pallas as pl
from jax.experimental.pallas import tpu as pltpu
from jax.sharding import PartitionSpec as P

NSLOW = 128
NSRC = 2
PERIOD = 4096
MIRROR = NSLOW // 2
TILE = 8
LANES = 128
NEAR = 4


def tables(bins):
    lag_total = 2 * bins
    lag = np.arange(lag_total)[:, None]
    freq = np.arange(bins)[None, :]
    theta = (lag * freq % lag_total) * (2.0 * math.pi / lag_total)
    cosine, sine = np.cos(theta), np.sin(theta)
    lower = np.concatenate([cosine[bins : bins + 1], sine[1:bins]], 0)
    inverse = np.concatenate([cosine[:bins], lower], 0) / math.sqrt(bins)
    order = np.concatenate([np.arange(bins), [bins], np.arange(lag_total - 1, bins, -1)])
    cosine, sine = cosine[order], sine[order]
    block = LANES // (2 * NSRC)
    parts = np.stack([cosine, -sine], 1).reshape(lag_total, 2, bins // block, block).transpose(0, 2, 1, 3)
    forward = np.repeat(parts[:, :, :, None], NSRC, 3).reshape(lag_total, -1) / math.sqrt(lag_total)
    return (
        inverse.astype(np.float32).astype(jnp.bfloat16),
        forward.astype(np.float32).astype(jnp.bfloat16),
    )


def cos_sin(steps, period):
    quarter = period // 4
    place = steps & (period - 1)
    quadrant = (place + quarter // 2) // quarter
    x = (place - quadrant * quarter).astype(jnp.float32) * (2.0 * math.pi / period)
    y = x * x
    sine = x * (1.0 + y * (-1.0 / 6 + y * (1.0 / 120 - y * (1.0 / 5040))))
    cosine = 1.0 + y * (-0.5 + y * (1.0 / 24 + y * (-1.0 / 720 + y * (1.0 / 40320))))
    odd = (quadrant & 1) == 1
    first = jnp.where(odd, sine, cosine)
    second = jnp.where(odd, cosine, sine)
    first = jnp.where(((quadrant + 1) & 2) == 2, -first, first)
    second = jnp.where((quadrant & 2) == 2, -second, second)
    return first, second


def exchange(source, target, send_sem, recv_sem, day, chan):
    return pltpu.make_async_remote_copy(
        src_ref=source,
        dst_ref=target,
        send_sem=send_sem,
        recv_sem=recv_sem,
        device_id={"days": day, "chan": chan},
        device_id_type=pl.DeviceIdType.MESH,
    )


def pack_halves(spectra_ref, kept, sent, day):
    count, depth, width = spectra_ref.shape
    half = width // 2
    left = lax.broadcasted_iota(jnp.int32, (depth, width), 1) < half
    upper = jnp.full((depth, width), day, jnp.int32) == 1
    for pair in range(count // 2):
        first = spectra_ref[2 * pair].astype(jnp.float32)
        second = spectra_ref[2 * pair + 1].astype(jnp.float32)
        lows = jnp.where(left, first, pltpu.roll(second, half, 1))
        highs = jnp.where(left, pltpu.roll(first, half, 1), second)
        kept[pair] = jnp.where(upper, highs, lows).astype(jnp.bfloat16)
        sent[pair] = jnp.where(upper, lows, highs).astype(jnp.bfloat16)


def source_columns(spectra_ref, sources_ref, chan):
    count, depth, width = spectra_ref.shape
    shape = (count * NSRC, width)
    row = lax.broadcasted_iota(jnp.int32, shape, 0)
    channel = lax.broadcasted_iota(jnp.int32, shape, 1) + chan * width
    wanted = jnp.zeros(shape, jnp.int32)
    for s in range(NSRC):
        wanted = jnp.where(row % NSRC == s, sources_ref[s], wanted)
    total = 0.0
    for w in range(count):
        pick = ((channel == wanted) & (row // NSRC == w)).astype(jnp.float32).astype(jnp.bfloat16)
        total = total + lax.dot_general(
            pick, spectra_ref[w], (((1,), (1,)), ((), ())), preferred_element_type=jnp.float32
        )
    return total.astype(jnp.bfloat16)


def correlate(x_ref, source_rows, inverse_ref, analytic, first_slot):
    pairs, depth, width = x_ref.shape
    bins, half = depth // 2, width // 2
    wide = NSRC * width
    shape = (source_rows.shape[0], wide)
    rows = lax.broadcasted_iota(jnp.int32, shape, 0)
    lane = lax.broadcasted_iota(jnp.int32, shape, 1)
    for pair in range(pairs):
        wanted = (2 * pair + lane % width // half) * NSRC + lane // width
        pick = (rows == wanted).astype(jnp.float32).astype(jnp.bfloat16)
        source = lax.dot_general(
            source_rows, pick, (((0,), (0,)), ((), ())), preferred_element_type=jnp.float32
        )
        channel = x_ref[pair].astype(jnp.float32)
        channel = jnp.concatenate([channel] * NSRC, 1)
        real_s, imag_s = source[:bins], source[bins:]
        real_x, imag_x = channel[:bins], channel[bins:]
        real = (real_s * real_x + imag_s * imag_x).astype(jnp.bfloat16)
        imag = (real_s * imag_x - imag_s * real_x).astype(jnp.bfloat16)
        for piece, value in enumerate((real, imag)):
            analytic[first_slot + pair, piece] = jnp.dot(
                inverse_ref[...], value, preferred_element_type=jnp.float32
            )


def stack_sums(analytic, slots, start, block, bins, totals):
    for slot in slots:
        here, there = pl.ds(start, block), pl.ds(bins + start, block)
        cos_re, sin_re = analytic[slot, 0, here], analytic[slot, 0, there]
        cos_im, sin_im = analytic[slot, 1, here], analytic[slot, 1, there]
        corr = [cos_re - sin_im, cos_re + sin_im]
        hilb = [cos_im + sin_re, cos_im - sin_re]
        if start == 0:
            top = lax.broadcasted_iota(jnp.int32, cos_re.shape, 0) == 0
            corr = [jnp.where(top, cos_re, corr[0]), jnp.where(top, sin_re, corr[1])]
            hilb = [jnp.where(top, cos_im, hilb[0]), jnp.where(top, sin_im, hilb[1])]
        for side in range(2):
            linear, phase_re, phase_im = totals[side]
            over = jnp.minimum(lax.rsqrt(corr[side] * corr[side] + hilb[side] * hilb[side]), 2.0)
            totals[side] = (
                linear + corr[side], phase_re + corr[side] * over, phase_im + hilb[side] * over
            )
    return totals


def first_stacks(analytic, slots, held):
    bins = analytic.shape[2] // 2
    for start in range(0, bins, TILE):
        totals = stack_sums(analytic, slots, start, TILE, bins, [(0.0, 0.0, 0.0)] * 2)
        for side in range(2):
            for index, total in enumerate(totals[side]):
                held[index, pl.ds(side * bins + start, TILE)] = total


def last_stacks(analytic, slots, held, weighted, factor):
    bins, width = analytic.shape[2] // 2, analytic.shape[3] // NSRC
    half = width // 2
    near_side = lax.broadcasted_iota(jnp.int32, (TILE, width), 1) < half

    def fold(value):
        parts = []
        for s in range(NSRC):
            part = value[:, s * width : (s + 1) * width]
            parts.append(part + pltpu.roll(part, half, 1))
        return jnp.where(near_side, parts[0], parts[1])

    results = [[], []]
    for start in range(0, bins, TILE):
        totals = [
            tuple(held[index, pl.ds(side * bins + start, TILE)] for index in range(3)) for side in range(2)
        ]
        totals = stack_sums(analytic, slots, start, TILE, bins, totals)
        for side in range(2):
            linear, phase_re, phase_im = (fold(total) for total in totals[side])
            results[side].append(linear * (phase_re * phase_re + phase_im * phase_im) * factor)
            if start % (2 * TILE):
                pair = jnp.concatenate(results[side][-2:], 0).astype(jnp.bfloat16)
                weighted[pl.ds(side * bins + start - TILE, 2 * TILE)] = pair


def own_offsets(offset_ref, half, day):
    row = jnp.broadcast_to(offset_ref[...].reshape(1, 2 * half), (TILE, 2 * half))
    lane = lax.broadcasted_iota(jnp.int32, row.shape, 1)
    return jnp.where(lane // half == day, row, pltpu.roll(row, half, 1))


def phase_table(offsets, phases, first, last, half):
    period = 2 * PERIOD
    per = LANES // half
    sub = lax.broadcasted_iota(jnp.int32, (TILE, LANES), 0)
    lane = lax.broadcasted_iota(jnp.int32, (TILE, LANES), 1)
    side = lane // half
    odd = (2 * sub + 1) * offsets

    def group(number, carry):
        base = number * TILE
        jumps_cos, jumps_sin = cos_sin(((base + sub) * per + side) * (offsets * (2 * TILE)), period)
        for member in range(TILE):
            freq = (base + member) * per + side
            cosine, sine = cos_sin(odd * freq, period)
            jump_cos = jnp.broadcast_to(jumps_cos[member : member + 1], (TILE, LANES))
            jump_sin = jnp.broadcast_to(jumps_sin[member : member + 1], (TILE, LANES))
            twice = 2.0 * jump_cos
            now = [cosine, sine]
            before = [cosine * jump_cos + sine * jump_sin, sine * jump_cos - cosine * jump_sin]
            rows = [[], []]
            for step in range(MIRROR // TILE):
                for piece in range(2):
                    rows[piece].append(now[piece])
                    later = twice * now[piece] - before[piece]
                    before[piece], now[piece] = now[piece], later
            for piece in range(2):
                for step in range(0, MIRROR // TILE, 2):
                    tile = jnp.concatenate(rows[piece][step : step + 2], 0).astype(jnp.bfloat16)
                    phases[base + member, pl.ds(piece * MIRROR + step * TILE, 2 * TILE)] = tile
        return carry

    lax.fori_loop(first // TILE, last // TILE, group, 0)


def centre_table(offsets, centre, half, bins):
    block = LANES // (2 * NSRC)
    column = jnp.broadcast_to(offsets[:1].astype(jnp.float32), (LANES, LANES)).T[:half].astype(jnp.int32)
    lane = lax.broadcasted_iota(jnp.int32, (half, LANES), 1)
    freq = lane % block

    def one(number, carry):
        cosine, sine = cos_sin((number * block + freq) * (column * (NSLOW - 1)), 2 * PERIOD)
        centre[number, 0] = cosine
        centre[number, 1] = jnp.where(lane < LANES // 2, -sine, sine)
        return carry

    lax.fori_loop(0, bins // block, one, 0)


def mask_table(masks):
    block = masks.shape[0]
    lane = lax.broadcasted_iota(jnp.int32, masks.shape[1:], 1) % block
    for f in range(block):
        masks[f] = (lane == f).astype(jnp.float32).astype(jnp.bfloat16)


def turned_spectra(weighted, forward_ref, centre, spectra_out, half):
    block = LANES // (2 * NSRC)
    result = lax.dot_general(
        weighted[...], forward_ref[...], (((0,), (0,)), ((), ())), preferred_element_type=jnp.float32
    )
    own = lax.broadcasted_iota(jnp.int32, (half, LANES), 1) // block % NSRC == 0
    for number in range(spectra_out.shape[0]):
        part = result[:, number * LANES : (number + 1) * LANES]
        part = jnp.where(own, part[:half], part[half:])
        turned = part * centre[number, 0] + pltpu.roll(part, LANES // 2, 1) * centre[number, 1]
        spectra_out[number] = turned.astype(jnp.bfloat16)


def spread_blocks(turned, masks, spread, number, half):
    value = turned[number]
    for f in range(masks.shape[0]):
        for piece in range(0, half, 2 * TILE):
            place = f * half + piece
            spread[number, place : place + 2 * TILE] = value[piece : piece + 2 * TILE] * masks[f]


def slant(phases, spread, number, first, last, half):
    count = spread.shape[1] // LANES
    left = []
    for index in range(count):
        place = number * count + index
        left.append(
            jnp.concatenate([phases[place, first:last], phases[place, MIRROR + first : MIRROR + last]], 0)
        )
    result = jnp.dot(jnp.concatenate(left, 1), spread[number], preferred_element_type=jnp.float32)
    even, odd = result[: last - first], pltpu.roll(result[last - first :], LANES // 2, 1)
    odd = jnp.where(lax.broadcasted_iota(jnp.int32, odd.shape, 1) < LANES // 2, -odd, odd)
    return even - odd, even + odd


def kernel(
    windows, scaling, days, chans, spectra_hbm, sources_hbm, offset_hbm, inverse_hbm, forward_hbm, out_ref,
    kept, sent, got, column, columns_far, plane, columns_near, analytic, weighted, turned, centre, masks, spread, phases, held,
    spectra_ref, leaving, arriving, owned, landing, inverse_ref, forward_ref,
    sources_ref, offset_ref, table_sem,
    half_sem, far_sem, near_sem, leave_sem, own_sem,
):
    count, depth, width = spectra_ref.shape
    bins, half = depth // 2, width // 2
    far = chans // NEAR
    rows = NSLOW // chans
    day, chan = lax.axis_index("days"), lax.axis_index("chan")
    high, low = chan // NEAR, chan % NEAR
    table_copies = [
        pltpu.make_async_copy(inverse_hbm, inverse_ref, table_sem.at[0]),
        pltpu.make_async_copy(forward_hbm, forward_ref, table_sem.at[1]),
    ]
    near_peers = [
        (dd, dl, (day + dd) % days, (low + dl) % NEAR)
        for dd in range(days)
        for dl in range(NEAR)
        if dd or dl
    ]
    far_peers = [
        (dd, dh, (day + dd) % days, (high + dh) % far)
        for dd in range(days)
        for dh in range(far)
        if dd or dh
    ]
    barrier = pltpu.get_barrier_semaphore()
    greeted = 0
    for dd, dl, to_day, to_low in near_peers:
        pl.semaphore_signal(
            barrier, inc=1, device_id={"days": to_day, "chan": high * NEAR + to_low},
            device_id_type=pl.DeviceIdType.MESH,
        )
        greeted += 1
    for dd, dh, to_day, to_high in far_peers:
        if dh:
            pl.semaphore_signal(
                barrier, inc=1, device_id={"days": to_day, "chan": to_high * NEAR + low},
                device_id_type=pl.DeviceIdType.MESH,
            )
            greeted += 1
    spectra_copy = pltpu.make_async_copy(spectra_hbm, spectra_ref, table_sem.at[2])
    sources_copy = pltpu.make_async_copy(sources_hbm, sources_ref, table_sem.at[3])
    offset_copy = pltpu.make_async_copy(offset_hbm, offset_ref, table_sem.at[4])
    copies = [sources_copy, spectra_copy, offset_copy]
    for copy in copies + table_copies:
        copy.start()
    for copy in copies:
        copy.wait()
    column[...] = source_columns(spectra_ref, sources_ref, chan)
    pack_halves(spectra_ref, kept, sent, day)
    pl.semaphore_wait(barrier, greeted)

    far_copies = []
    for dd, dh, to_day, to_high in far_peers:
        if dd == 0:
            copy = exchange(
                column, columns_far.at[dh - 1], far_sem.at[0, dh - 1], far_sem.at[1, dh - 1],
                day, to_high * NEAR + low,
            )
            copy.start()
            far_copies.append(copy)
    half_copy = exchange(sent, got, half_sem.at[0], half_sem.at[1], (day + 1) % days, chan)
    half_copy.start()
    offsets = own_offsets(offset_ref, half, day)
    blocks = phases.shape[0]
    phase_table(offsets, phases, 0, blocks // 2, half)
    total = column[...].astype(jnp.float32)
    for index, copy in enumerate(far_copies):
        copy.wait_recv()
        total = total + columns_far[index].astype(jnp.float32)
    plane[...] = total.astype(jnp.bfloat16)
    near_copies = []
    for index, (dd, dl, to_day, to_low) in enumerate(near_peers):
        copy = exchange(
            plane, columns_near.at[index], near_sem.at[0, index], near_sem.at[1, index],
            to_day, high * NEAR + to_low,
        )
        copy.start()
        near_copies.append((dd, copy))
    phase_table(offsets, phases, blocks // 2, blocks, half)
    centre_table(offsets, centre, half, bins)
    mask_table(masks)

    def gather(wanted, value):
        for index, (dd, copy) in enumerate(near_copies):
            if dd == wanted:
                copy.wait_recv()
                value = value + columns_near[index].astype(jnp.float32)
        return value.astype(jnp.bfloat16)

    pairs = count // 2
    rows_own = gather(0, total)
    for copy in table_copies:
        copy.wait()
    correlate(kept, rows_own, inverse_ref, analytic, 0)
    first_stacks(analytic, range(pairs), held)
    rows_other = gather(1, 0.0)
    half_copy.wait_recv()
    correlate(got, rows_other, inverse_ref, analytic, pairs)
    others = range(pairs, 2 * pairs)
    last_stacks(analytic, others, held, weighted, scaling / windows**3)
    turned_spectra(weighted, forward_ref, centre, turned, half)

    wire = leaving.dtype
    blocks_own = turned.shape[0] // days
    leave_copies = []
    edge = max(1, 2 * TILE // (NEAR * rows))
    middle = MIRROR - edge * NEAR * rows

    def work(turn, first, last, spreading):
        target = (day + days - 1 - turn) % days
        for pair in range(blocks_own // 2):
            ends = []
            for at in range(2):
                number = target * blocks_own + 2 * pair + at
                if spreading:
                    spread_blocks(turned, masks, spread, number, half)
                ends.append(slant(phases, spread, number, first, last, half))
            for owner in range(chans):
                upper = owner * rows >= MIRROR
                begin = owner * rows - MIRROR if upper else MIRROR - (owner + 1) * rows
                if first <= begin < last:
                    both = [end[upper][begin - first : begin - first + rows] for end in ends]
                    leaving[target, owner % NEAR, owner // NEAR, pair] = jnp.concatenate(both, 0).astype(wire)

    def leave(turn, cut):
        shift = days - 1 - turn
        target = (day + shift) % days
        at, size = ((0, edge), (far - edge, edge), (edge, far - 2 * edge))[cut]
        for index, (dd, dl, to_day, to_low) in enumerate(near_peers):
            if dd == shift:
                copy = exchange(
                    leaving.at[target, to_low, pl.ds(at, size)], arriving.at[index, pl.ds(at, size)],
                    leave_sem.at[0, cut, index], leave_sem.at[1, cut, index],
                    target, high * NEAR + to_low,
                )
                copy.start()
                leave_copies.append((at, copy))

    for turn in range(days):
        work(turn, middle, MIRROR, True)
        leave(turn, 0)
    for turn in range(days):
        leave(turn, 1)
    for turn in range(days):
        work(turn, 0, middle, False)
        leave(turn, 2)
    for hi in range(far):
        total = leaving[day, low, hi].astype(jnp.float32)
        index = 0
        for at, copy in leave_copies:
            if at == hi:
                copy.wait_recv()
        for index in range(len(near_peers)):
            total = total + arriving[index, hi].astype(jnp.float32)
        owned[hi] = total.astype(wire)
        step = (hi - high) % far
        for dd in range(days):
            def send(dd=dd, hi=hi, step=step):
                exchange(
                    owned.at[hi], landing.at[dd, step], own_sem.at[0, dd, step], own_sem.at[1, dd, step],
                    (day + dd) % days, hi * NEAR + low,
                ).start()

            if dd:
                send()
            else:
                pl.when(step != 0)(send)

    def landed(dd, dh):
        return exchange(
            owned.at[0], landing.at[dd, dh], own_sem.at[0, dd, dh], own_sem.at[1, dd, dh],
            (day + dd) % days, (high + dh) % far * NEAR + low,
        )

    block = LANES // (2 * NSRC)
    for dd in range(days):
        total = 0.0
        for dh in range(far):
            if dd or dh:
                landed(dd, dh).wait_recv()
                total = total + landing[dd, dh].astype(jnp.float32)
            else:
                total = owned[high].astype(jnp.float32)
        pieces = [total[pair, at * rows : (at + 1) * rows] for pair in range(blocks_own // 2) for at in range(2)]
        for part in range(blocks_own * block // LANES):
            some = pieces[part * LANES // block : (part + 1) * LANES // block]
            for s in range(NSRC):
                for p in range(2):
                    begin = (p * NSRC + s) * block
                    value = jnp.concatenate([piece[:, begin : begin + block] for piece in some], 1)
                    mirrored = jnp.concatenate([value[row : row + 1] for row in reversed(range(rows))], 0)
                    lower = jnp.full(value.shape, chan * rows, jnp.int32) < MIRROR
                    out_ref[s, p, (day + dd) % days, part] = jnp.where(lower, mirrored, value)
    half_copy.wait_send()
    for copy in far_copies:
        copy.wait_send()
    for dd, copy in near_copies:
        copy.wait_send()
    for hi, copy in leave_copies:
        copy.wait_send()
    for dd in range(days):
        for dh in range(far):
            if dd or dh:
                landed(dd, dh).wait_send()


def shards(spectra, sources, offsets):
    count, depth, width = spectra.shape
    bins, half = depth // 2, width // 2
    days, chans = lax.axis_size("days"), lax.axis_size("chan")
    windows = count * days
    inverse, forward = tables(bins)
    scaling = windows**1.5 / math.sqrt(width * chans)
    far, rows, pairs = chans // NEAR, NSLOW // chans, count // 2
    near_count = days * NEAR - 1
    wire = jnp.bfloat16 if rows % TILE == 0 else jnp.float32
    block = LANES // (2 * NSRC)
    blocks = bins // block
    chunk = (blocks // days // 2, 2 * rows, LANES)
    parts = bins // days // LANES
    vmem = pl.BlockSpec(memory_space=pltpu.VMEM)
    hbm = pl.BlockSpec(memory_space=pltpu.HBM)
    bf16, f32 = jnp.bfloat16, jnp.float32
    dma = pltpu.SemaphoreType.DMA
    out = pl.pallas_call(
        functools.partial(kernel, windows, scaling, days, chans),
        out_shape=pltpu.VMEM((NSRC, 2, days, parts, rows, LANES), f32),
        in_specs=[hbm] * 5,
        out_specs=vmem,
        scratch_shapes=[
            pltpu.VMEM((pairs, depth, width), bf16),
            pltpu.VMEM((pairs, depth, width), bf16),
            pltpu.VMEM((pairs, depth, width), bf16),
            pltpu.VMEM((count * NSRC, depth), bf16),
            pltpu.VMEM((far - 1, count * NSRC, depth), bf16),
            pltpu.VMEM((count * NSRC, depth), bf16),
            pltpu.VMEM((near_count, count * NSRC, depth), bf16),
            pltpu.VMEM((2 * pairs, 2, depth, NSRC * width), f32),
            pltpu.VMEM((depth, width), bf16),
            pltpu.VMEM((blocks, half, LANES), bf16),
            pltpu.VMEM((blocks, 2, half, LANES), f32),
            pltpu.VMEM((block, 2 * TILE, LANES), bf16),
            pltpu.VMEM((blocks, block * half, LANES), bf16),
            pltpu.VMEM((bins * half // LANES, NSLOW, LANES), bf16),
            pltpu.VMEM((3, depth, NSRC * width), f32),
            pltpu.VMEM((count, depth, width), bf16),
            pltpu.VMEM((days, NEAR, far) + chunk, wire),
            pltpu.VMEM((near_count, far) + chunk, wire),
            pltpu.VMEM((far,) + chunk, wire),
            pltpu.VMEM((days, far) + chunk, wire),
            pltpu.VMEM(inverse.shape, bf16),
            pltpu.VMEM(forward.shape, bf16),
            pltpu.SMEM(sources.shape, jnp.int32),
            pltpu.VMEM(offsets.shape, jnp.int32),
            dma((5,)),
            dma((2,)),
            dma((2, far - 1)),
            dma((2, near_count)),
            dma((2, 3, near_count)),
            dma((2, days, far)),
        ],
        compiler_params=pltpu.CompilerParams(
            collective_id=0, has_side_effects=True, vmem_limit_bytes=56 * 1024 * 1024
        ),
    )(spectra, sources, offsets, jnp.asarray(inverse), jnp.asarray(forward))
    return out.transpose(4, 0, 1, 2, 3, 5).reshape(rows, NSRC, 2, bins)


def solution(mesh):
    placed = (P("days", None, "chan"), P(), P("chan"))
    return jax.shard_map(
        shards, mesh=mesh, in_specs=placed, out_specs=P("chan", None, None, None), check_vma=False
    )
```

```python
import functools
import math

import jax
import jax.numpy as jnp
import numpy as np
from jax import lax
from jax.experimental import pallas as pl
from jax.experimental.pallas import tpu as pltpu
from jax.sharding import PartitionSpec as P

NSLOW = 128
NSRC = 2
PERIOD = 4096
MIRROR = NSLOW // 2
TILE = 8
LANES = 128
NEAR = 4


def tables(bins):
    lag_total = 2 * bins
    lag = np.arange(lag_total)[:, None]
    freq = np.arange(bins)[None, :]
    theta = (lag * freq % lag_total) * (2.0 * math.pi / lag_total)
    cosine, sine = np.cos(theta), np.sin(theta)
    lower = np.concatenate([cosine[bins : bins + 1], sine[1:bins]], 0)
    inverse = np.concatenate([cosine[:bins], lower], 0) / math.sqrt(bins)
    order = np.concatenate([np.arange(bins), [bins], np.arange(lag_total - 1, bins, -1)])
    order = order.reshape(2, 2, -1).transpose(1, 0, 2).reshape(-1)
    cosine, sine = cosine[order], sine[order]
    block = LANES // (2 * NSRC)
    parts = np.stack([cosine, -sine], 1).reshape(lag_total, 2, bins // block, block).transpose(0, 2, 1, 3)
    forward = np.repeat(parts[:, :, :, None], NSRC, 3).reshape(lag_total, -1) / math.sqrt(lag_total)
    return (
        inverse.astype(np.float32).astype(jnp.bfloat16),
        forward.astype(np.float32).astype(jnp.bfloat16),
    )


def cos_sin(steps, period):
    quarter = period // 4
    place = steps & (period - 1)
    quadrant = (place + quarter // 2) // quarter
    x = (place - quadrant * quarter).astype(jnp.float32) * (2.0 * math.pi / period)
    y = x * x
    sine = x * (1.0 + y * (-1.0 / 6 + y * (1.0 / 120 - y * (1.0 / 5040))))
    cosine = 1.0 + y * (-0.5 + y * (1.0 / 24 + y * (-1.0 / 720 + y * (1.0 / 40320))))
    odd = (quadrant & 1) == 1
    first = jnp.where(odd, sine, cosine)
    second = jnp.where(odd, cosine, sine)
    first = jnp.where(((quadrant + 1) & 2) == 2, -first, first)
    second = jnp.where((quadrant & 2) == 2, -second, second)
    return first, second


def exchange(source, target, send_sem, recv_sem, day, chan):
    return pltpu.make_async_remote_copy(
        src_ref=source,
        dst_ref=target,
        send_sem=send_sem,
        recv_sem=recv_sem,
        device_id={"days": day, "chan": chan},
        device_id_type=pl.DeviceIdType.MESH,
    )


def pack_halves(spectra_ref, kept, sent, day):
    count, depth, width = spectra_ref.shape
    half = width // 2
    left = lax.broadcasted_iota(jnp.int32, (depth, width), 1) < half
    upper = jnp.full((depth, width), day, jnp.int32) == 1
    for pair in range(count // 2):
        first = spectra_ref[2 * pair].astype(jnp.float32)
        second = spectra_ref[2 * pair + 1].astype(jnp.float32)
        lows = jnp.where(left, first, pltpu.roll(second, half, 1))
        highs = jnp.where(left, pltpu.roll(first, half, 1), second)
        kept[pair] = jnp.where(upper, highs, lows).astype(jnp.bfloat16)
        sent[pair] = jnp.where(upper, lows, highs).astype(jnp.bfloat16)


def source_columns(spectra_ref, sources_ref, chan):
    count, depth, width = spectra_ref.shape
    shape = (count * NSRC, width)
    row = lax.broadcasted_iota(jnp.int32, shape, 0)
    channel = lax.broadcasted_iota(jnp.int32, shape, 1) + chan * width
    wanted = jnp.zeros(shape, jnp.int32)
    for s in range(NSRC):
        wanted = jnp.where(row % NSRC == s, sources_ref[s], wanted)
    total = 0.0
    for w in range(count):
        pick = ((channel == wanted) & (row // NSRC == w)).astype(jnp.float32).astype(jnp.bfloat16)
        total = total + lax.dot_general(
            pick, spectra_ref[w], (((1,), (1,)), ((), ())), preferred_element_type=jnp.float32
        )
    return total.astype(jnp.bfloat16)


def correlate(x_ref, source_rows, inverse_ref, analytic, first_slot, pairs):
    depth, width = x_ref.shape[1:]
    bins, half = depth // 2, width // 2
    wide = NSRC * width
    shape = (source_rows.shape[0], wide)
    rows = lax.broadcasted_iota(jnp.int32, shape, 0)
    lane = lax.broadcasted_iota(jnp.int32, shape, 1)
    for pair in pairs:
        wanted = (2 * pair + lane % width // half) * NSRC + lane // width
        pick = (rows == wanted).astype(jnp.float32).astype(jnp.bfloat16)
        source = lax.dot_general(
            source_rows, pick, (((0,), (0,)), ((), ())), preferred_element_type=jnp.float32
        )
        channel = x_ref[pair].astype(jnp.float32)
        channel = jnp.concatenate([channel] * NSRC, 1)
        real_s, imag_s = source[:bins], source[bins:]
        real_x, imag_x = channel[:bins], channel[bins:]
        real = (real_s * real_x + imag_s * imag_x).astype(jnp.bfloat16)
        imag = (real_s * imag_x - imag_s * real_x).astype(jnp.bfloat16)
        for piece, value in enumerate((real, imag)):
            analytic[first_slot + pair, piece] = jnp.dot(
                inverse_ref[...], value, preferred_element_type=jnp.float32
            )


def stack_sums(analytic, slots, start, block, bins, totals):
    for slot in slots:
        here, there = pl.ds(start, block), pl.ds(bins + start, block)
        cos_re, sin_re = analytic[slot, 0, here], analytic[slot, 0, there]
        cos_im, sin_im = analytic[slot, 1, here], analytic[slot, 1, there]
        corr = [cos_re - sin_im, cos_re + sin_im]
        hilb = [cos_im + sin_re, cos_im - sin_re]
        if start == 0:
            top = lax.broadcasted_iota(jnp.int32, cos_re.shape, 0) == 0
            corr = [jnp.where(top, cos_re, corr[0]), jnp.where(top, sin_re, corr[1])]
            hilb = [jnp.where(top, cos_im, hilb[0]), jnp.where(top, sin_im, hilb[1])]
        for side in range(2):
            linear, phase_re, phase_im = totals[side]
            over = jnp.minimum(lax.rsqrt(corr[side] * corr[side] + hilb[side] * hilb[side]), 2.0)
            totals[side] = (
                linear + corr[side], phase_re + corr[side] * over, phase_im + hilb[side] * over
            )
    return totals


def first_stacks(analytic, slots, held):
    bins = analytic.shape[2] // 2
    for start in range(0, bins, TILE):
        totals = stack_sums(analytic, slots, start, TILE, bins, [(0.0, 0.0, 0.0)] * 2)
        for side in range(2):
            for index, total in enumerate(totals[side]):
                held[index, pl.ds(side * bins + start, TILE)] = total


def last_stacks(analytic, slots, held, weighted, factor, forward_ref):
    bins, width = analytic.shape[2] // 2, analytic.shape[3] // NSRC
    half = width // 2
    near_side = lax.broadcasted_iota(jnp.int32, (TILE, width), 1) < half

    def fold(value):
        parts = []
        for s in range(NSRC):
            part = value[:, s * width : (s + 1) * width]
            parts.append(part + pltpu.roll(part, half, 1))
        return jnp.where(near_side, parts[0], parts[1])

    results = [[], []]
    spectrum = 0.0
    part = bins // 2
    for start in range(0, bins, TILE):
        totals = [
            tuple(held[index, pl.ds(side * bins + start, TILE)] for index in range(3)) for side in range(2)
        ]
        totals = stack_sums(analytic, slots, start, TILE, bins, totals)
        for side in range(2):
            linear, phase_re, phase_im = (fold(total) for total in totals[side])
            results[side].append(linear * (phase_re * phase_re + phase_im * phase_im) * factor)
            if start % (2 * TILE):
                pair = jnp.concatenate(results[side][-2:], 0).astype(jnp.bfloat16)
                weighted[pl.ds(start // part * bins + side * part + start % part - TILE, 2 * TILE)] = pair
        if (start + TILE) % part == 0:
            here = pl.ds(start // part * bins, bins)
            spectrum = spectrum + lax.dot_general(
                weighted[here], forward_ref[here], (((0,), (0,)), ((), ())), preferred_element_type=jnp.float32
            )
    return spectrum


def own_offsets(offset_ref, half, day):
    row = jnp.broadcast_to(offset_ref[...].reshape(1, 2 * half), (TILE, 2 * half))
    lane = lax.broadcasted_iota(jnp.int32, row.shape, 1)
    return jnp.where(lane // half == day, row, pltpu.roll(row, half, 1))


def phase_table(offsets, phases, first, last, half):
    period = 2 * PERIOD
    per = LANES // half
    sub = lax.broadcasted_iota(jnp.int32, (TILE, LANES), 0)
    lane = lax.broadcasted_iota(jnp.int32, (TILE, LANES), 1)
    side = lane // half
    odd = (2 * sub + 1) * offsets

    def group(number, carry):
        base = number * TILE
        jumps_cos, jumps_sin = cos_sin(((base + sub) * per + side) * (offsets * (2 * TILE)), period)
        for member in range(TILE):
            freq = (base + member) * per + side
            cosine, sine = cos_sin(odd * freq, period)
            jump_cos = jnp.broadcast_to(jumps_cos[member : member + 1], (TILE, LANES))
            jump_sin = jnp.broadcast_to(jumps_sin[member : member + 1], (TILE, LANES))
            twice = 2.0 * jump_cos
            now = [cosine, sine]
            before = [cosine * jump_cos + sine * jump_sin, sine * jump_cos - cosine * jump_sin]
            rows = [[], []]
            for step in range(MIRROR // TILE):
                for piece in range(2):
                    rows[piece].append(now[piece])
                    later = twice * now[piece] - before[piece]
                    before[piece], now[piece] = now[piece], later
            for piece in range(2):
                for step in range(0, MIRROR // TILE, 2):
                    tile = jnp.concatenate(rows[piece][step : step + 2], 0).astype(jnp.bfloat16)
                    phases[base + member, pl.ds(piece * MIRROR + step * TILE, 2 * TILE)] = tile
        return carry

    lax.fori_loop(first // TILE, last // TILE, group, 0)


def centre_table(offsets, centre, half, bins):
    block = LANES // (2 * NSRC)
    column = jnp.broadcast_to(offsets[:1].astype(jnp.float32), (LANES, LANES)).T[:half].astype(jnp.int32)
    lane = lax.broadcasted_iota(jnp.int32, (half, LANES), 1)
    freq = lane % block

    def one(number, carry):
        cosine, sine = cos_sin((number * block + freq) * (column * (NSLOW - 1)), 2 * PERIOD)
        centre[number, 0] = cosine
        centre[number, 1] = jnp.where(lane < LANES // 2, -sine, sine)
        return carry

    lax.fori_loop(0, bins // block, one, 0)


def mask_table(masks):
    block = masks.shape[0]
    lane = lax.broadcasted_iota(jnp.int32, masks.shape[1:], 1) % block
    for f in range(block):
        masks[f] = (lane == f).astype(jnp.float32).astype(jnp.bfloat16)


def turned_spectra(result, centre, spectra_out, half):
    block = LANES // (2 * NSRC)
    own = lax.broadcasted_iota(jnp.int32, (half, LANES), 1) // block % NSRC == 0
    for number in range(spectra_out.shape[0]):
        part = result[:, number * LANES : (number + 1) * LANES]
        part = jnp.where(own, part[:half], part[half:])
        turned = part * centre[number, 0] + pltpu.roll(part, LANES // 2, 1) * centre[number, 1]
        spectra_out[number] = turned.astype(jnp.bfloat16)


def spread_blocks(turned, masks, spread, number, half):
    value = turned[number]
    for f in range(masks.shape[0]):
        for piece in range(0, half, 2 * TILE):
            place = f * half + piece
            spread[number, place : place + 2 * TILE] = value[piece : piece + 2 * TILE] * masks[f]


def slant(phases, spread, number, first, last, half):
    count = spread.shape[1] // LANES
    left = []
    for index in range(count):
        place = number * count + index
        left.append(
            jnp.concatenate([phases[place, first:last], phases[place, MIRROR + first : MIRROR + last]], 0)
        )
    result = jnp.dot(jnp.concatenate(left, 1), spread[number], preferred_element_type=jnp.float32)
    even, odd = result[: last - first], pltpu.roll(result[last - first :], LANES // 2, 1)
    odd = jnp.where(lax.broadcasted_iota(jnp.int32, odd.shape, 1) < LANES // 2, -odd, odd)
    return even - odd, even + odd


def kernel(
    windows, scaling, days, chans, spectra_hbm, sources_hbm, offset_hbm, inverse_hbm, forward_hbm, out_ref,
    kept, sent, got, column, columns_far, plane, columns_near, analytic, weighted, turned, centre, masks, spread, phases, held,
    spectra_ref, leaving, arriving, owned, landing, inverse_ref, forward_ref,
    sources_ref, offset_ref, table_sem,
    half_sem, far_sem, near_sem, leave_sem, own_sem,
):
    count, depth, width = spectra_ref.shape
    bins, half = depth // 2, width // 2
    far = chans // NEAR
    rows = NSLOW // chans
    day, chan = lax.axis_index("days"), lax.axis_index("chan")
    high, low = chan // NEAR, chan % NEAR
    table_copies = [
        pltpu.make_async_copy(inverse_hbm, inverse_ref, table_sem.at[0]),
        pltpu.make_async_copy(forward_hbm, forward_ref, table_sem.at[1]),
    ]
    near_peers = [
        (dd, dl, (day + dd) % days, (low + dl) % NEAR)
        for dd in range(days)
        for dl in range(NEAR)
        if dd or dl
    ]
    far_peers = [
        (dd, dh, (day + dd) % days, (high + dh) % far)
        for dd in range(days)
        for dh in range(far)
        if dd or dh
    ]
    barrier = pltpu.get_barrier_semaphore()
    greeted = 0
    for dd, dl, to_day, to_low in near_peers:
        pl.semaphore_signal(
            barrier, inc=1, device_id={"days": to_day, "chan": high * NEAR + to_low},
            device_id_type=pl.DeviceIdType.MESH,
        )
        greeted += 1
    for dd, dh, to_day, to_high in far_peers:
        if dh and not dd:
            pl.semaphore_signal(
                barrier, inc=1, device_id={"days": to_day, "chan": to_high * NEAR + low},
                device_id_type=pl.DeviceIdType.MESH,
            )
            greeted += 1
    spectra_copy = pltpu.make_async_copy(spectra_hbm, spectra_ref, table_sem.at[2])
    sources_copy = pltpu.make_async_copy(sources_hbm, sources_ref, table_sem.at[3])
    offset_copy = pltpu.make_async_copy(offset_hbm, offset_ref, table_sem.at[4])
    copies = [sources_copy, spectra_copy, offset_copy]
    for copy in copies + table_copies:
        copy.start()
    for copy in copies:
        copy.wait()
    column[...] = source_columns(spectra_ref, sources_ref, chan)
    pack_halves(spectra_ref, kept, sent, day)
    pl.semaphore_wait(barrier, greeted)

    far_copies = []
    for dd, dh, to_day, to_high in far_peers:
        if dd == 0:
            copy = exchange(
                column, columns_far.at[dh - 1], far_sem.at[0, dh - 1], far_sem.at[1, dh - 1],
                day, to_high * NEAR + low,
            )
            copy.start()
            far_copies.append(copy)
    half_copies = []
    for pair in range(count // 2):
        half_copies.append(exchange(
            sent.at[pair], got.at[pair], half_sem.at[0, pair], half_sem.at[1, pair], (day + 1) % days, chan
        ))
    half_copies[0].start()
    offsets = own_offsets(offset_ref, half, day)
    blocks = phases.shape[0]
    phase_table(offsets, phases, 0, blocks // 2, half)
    total = column[...].astype(jnp.float32)
    for index, copy in enumerate(far_copies):
        copy.wait_recv()
        total = total + columns_far[index].astype(jnp.float32)
    plane[...] = total.astype(jnp.bfloat16)
    near_copies = []
    for index, (dd, dl, to_day, to_low) in enumerate(near_peers):
        copy = exchange(
            plane, columns_near.at[index], near_sem.at[0, index], near_sem.at[1, index],
            to_day, high * NEAR + to_low,
        )
        copy.start()
        near_copies.append((dd, copy))
    half_copies[1].start()
    phase_table(offsets, phases, blocks // 2, blocks, half)
    centre_table(offsets, centre, half, bins)
    mask_table(masks)

    def gather(wanted, value):
        for index, (dd, copy) in enumerate(near_copies):
            if dd == wanted:
                copy.wait_recv()
                value = value + columns_near[index].astype(jnp.float32)
        return value.astype(jnp.bfloat16)

    pairs = count // 2
    rows_own = gather(0, total)
    for copy in table_copies:
        copy.wait()
    correlate(kept, rows_own, inverse_ref, analytic, 0, range(pairs))
    first_stacks(analytic, range(pairs), held)
    rows_other = gather(1, 0.0)
    for pair, copy in enumerate(half_copies):
        copy.wait_recv()
        correlate(got, rows_other, inverse_ref, analytic, pairs, [pair])
    others = range(pairs, 2 * pairs)
    spectrum = last_stacks(analytic, others, held, weighted, scaling / windows**3, forward_ref)
    turned_spectra(spectrum, centre, turned, half)

    wire = leaving.dtype
    blocks_own = turned.shape[0] // days
    leave_copies = []
    edge = max(1, 2 * TILE // (NEAR * rows))
    middle = MIRROR - edge * NEAR * rows

    def work(turn, first, last, spreading):
        target = (day + days - 1 - turn) % days
        for pair in range(blocks_own // 2):
            ends = []
            for at in range(2):
                number = target * blocks_own + 2 * pair + at
                if spreading:
                    spread_blocks(turned, masks, spread, number, half)
                ends.append(slant(phases, spread, number, first, last, half))
            for owner in range(chans):
                upper = owner * rows >= MIRROR
                begin = owner * rows - MIRROR if upper else MIRROR - (owner + 1) * rows
                if first <= begin < last:
                    both = [end[upper][begin - first : begin - first + rows] for end in ends]
                    leaving[target, owner % NEAR, owner // NEAR, pair] = jnp.concatenate(both, 0).astype(wire)

    def leave(turn, cut):
        shift = days - 1 - turn
        target = (day + shift) % days
        at, size = ((0, edge), (far - edge, edge), (edge, far - 2 * edge))[cut]
        for index, (dd, dl, to_day, to_low) in enumerate(near_peers):
            if dd == shift:
                copy = exchange(
                    leaving.at[target, to_low, pl.ds(at, size)], arriving.at[index, pl.ds(at, size)],
                    leave_sem.at[0, cut, index], leave_sem.at[1, cut, index],
                    target, high * NEAR + to_low,
                )
                copy.start()
                leave_copies.append((at, copy))

    for turn in range(days):
        work(turn, middle, MIRROR, True)
        leave(turn, 0)
    for turn in range(days):
        leave(turn, 1)
    for turn in range(days):
        work(turn, 0, middle, False)
        leave(turn, 2)
    for hi in range(far):
        total = leaving[day, low, hi].astype(jnp.float32)
        index = 0
        for at, copy in leave_copies:
            if at == hi:
                copy.wait_recv()
        for index in range(len(near_peers)):
            total = total + arriving[index, hi].astype(jnp.float32)
        owned[hi] = total.astype(wire)
        step = (hi - high) % far
        for dd in range(days):
            def send(dd=dd, hi=hi, step=step):
                exchange(
                    owned.at[hi], landing.at[dd, step], own_sem.at[0, dd, step], own_sem.at[1, dd, step],
                    (day + dd) % days, hi * NEAR + low,
                ).start()

            if dd:
                send()
            else:
                pl.when(step != 0)(send)

    def landed(dd, dh):
        return exchange(
            owned.at[0], landing.at[dd, dh], own_sem.at[0, dd, dh], own_sem.at[1, dd, dh],
            (day + dd) % days, (high + dh) % far * NEAR + low,
        )

    block = LANES // (2 * NSRC)
    for dd in range(days):
        total = 0.0
        for dh in range(far):
            if dd or dh:
                landed(dd, dh).wait_recv()
                total = total + landing[dd, dh].astype(jnp.float32)
            else:
                total = owned[high].astype(jnp.float32)
        pieces = [total[pair, at * rows : (at + 1) * rows] for pair in range(blocks_own // 2) for at in range(2)]
        for part in range(blocks_own * block // LANES):
            some = pieces[part * LANES // block : (part + 1) * LANES // block]
            for s in range(NSRC):
                for p in range(2):
                    begin = (p * NSRC + s) * block
                    value = jnp.concatenate([piece[:, begin : begin + block] for piece in some], 1)
                    mirrored = jnp.concatenate([value[row : row + 1] for row in reversed(range(rows))], 0)
                    lower = jnp.full(value.shape, chan * rows, jnp.int32) < MIRROR
                    out_ref[s, p, (day + dd) % days, part] = jnp.where(lower, mirrored, value)
    for copy in half_copies:
        copy.wait_send()
    for copy in far_copies:
        copy.wait_send()
    for dd, copy in near_copies:
        copy.wait_send()
    for hi, copy in leave_copies:
        copy.wait_send()
    for dd in range(days):
        for dh in range(far):
            if dd or dh:
                landed(dd, dh).wait_send()


def shards(spectra, sources, offsets):
    count, depth, width = spectra.shape
    bins, half = depth // 2, width // 2
    days, chans = lax.axis_size("days"), lax.axis_size("chan")
    windows = count * days
    inverse, forward = tables(bins)
    scaling = windows**1.5 / math.sqrt(width * chans)
    far, rows, pairs = chans // NEAR, NSLOW // chans, count // 2
    near_count = days * NEAR - 1
    wire = jnp.bfloat16 if rows % TILE == 0 else jnp.float32
    block = LANES // (2 * NSRC)
    blocks = bins // block
    chunk = (blocks // days // 2, 2 * rows, LANES)
    parts = bins // days // LANES
    vmem = pl.BlockSpec(memory_space=pltpu.VMEM)
    hbm = pl.BlockSpec(memory_space=pltpu.HBM)
    bf16, f32 = jnp.bfloat16, jnp.float32
    dma = pltpu.SemaphoreType.DMA
    out = pl.pallas_call(
        functools.partial(kernel, windows, scaling, days, chans),
        out_shape=pltpu.VMEM((NSRC, 2, days, parts, rows, LANES), f32),
        in_specs=[hbm] * 5,
        out_specs=vmem,
        scratch_shapes=[
            pltpu.VMEM((pairs, depth, width), bf16),
            pltpu.VMEM((pairs, depth, width), bf16),
            pltpu.VMEM((pairs, depth, width), bf16),
            pltpu.VMEM((count * NSRC, depth), bf16),
            pltpu.VMEM((far - 1, count * NSRC, depth), bf16),
            pltpu.VMEM((count * NSRC, depth), bf16),
            pltpu.VMEM((near_count, count * NSRC, depth), bf16),
            pltpu.VMEM((2 * pairs, 2, depth, NSRC * width), f32),
            pltpu.VMEM((depth, width), bf16),
            pltpu.VMEM((blocks, half, LANES), bf16),
            pltpu.VMEM((blocks, 2, half, LANES), f32),
            pltpu.VMEM((block, 2 * TILE, LANES), bf16),
            pltpu.VMEM((blocks, block * half, LANES), bf16),
            pltpu.VMEM((bins * half // LANES, NSLOW, LANES), bf16),
            pltpu.VMEM((3, depth, NSRC * width), f32),
            pltpu.VMEM((count, depth, width), bf16),
            pltpu.VMEM((days, NEAR, far) + chunk, wire),
            pltpu.VMEM((near_count, far) + chunk, wire),
            pltpu.VMEM((far,) + chunk, wire),
            pltpu.VMEM((days, far) + chunk, wire),
            pltpu.VMEM(inverse.shape, bf16),
            pltpu.VMEM(forward.shape, bf16),
            pltpu.SMEM(sources.shape, jnp.int32),
            pltpu.VMEM(offsets.shape, jnp.int32),
            dma((5,)),
            dma((2, pairs)),
            dma((2, far - 1)),
            dma((2, near_count)),
            dma((2, 3, near_count)),
            dma((2, days, far)),
        ],
        compiler_params=pltpu.CompilerParams(
            collective_id=0, has_side_effects=True, vmem_limit_bytes=56 * 1024 * 1024
        ),
    )(spectra, sources, offsets, jnp.asarray(inverse), jnp.asarray(forward))
    return out.transpose(4, 0, 1, 2, 3, 5).reshape(rows, NSRC, 2, bins)


def solution(mesh):
    placed = (P("days", None, "chan"), P(), P("chan"))
    return jax.shard_map(
        shards, mesh=mesh, in_specs=placed, out_specs=P("chan", None, None, None), check_vma=False
    )
```

```python
import functools
import math

import jax
import jax.numpy as jnp
import numpy as np
from jax import lax
from jax.experimental import pallas as pl
from jax.experimental.pallas import tpu as pltpu
from jax.sharding import PartitionSpec as P

NSLOW = 128
NSRC = 2
PERIOD = 4096
MIRROR = NSLOW // 2
TILE = 8
LANES = 128
NEAR = 4


def tables(bins):
    lag_total = 2 * bins
    lag = np.arange(lag_total)[:, None]
    freq = np.arange(bins)[None, :]
    theta = (lag * freq % lag_total) * (2.0 * math.pi / lag_total)
    cosine, sine = np.cos(theta), np.sin(theta)
    lower = np.concatenate([cosine[bins : bins + 1], sine[1:bins]], 0)
    inverse = np.concatenate([cosine[:bins], lower], 0) / math.sqrt(bins)
    order = np.concatenate([np.arange(bins), [bins], np.arange(lag_total - 1, bins, -1)])
    order = order.reshape(2, 2, -1).transpose(1, 0, 2).reshape(-1)
    cosine, sine = cosine[order], sine[order]
    block = LANES // (2 * NSRC)
    parts = np.stack([cosine, -sine], 1).reshape(lag_total, 2, -1, NSRC, block).transpose(0, 2, 1, 3, 4)
    forward = parts.reshape(lag_total, -1) / math.sqrt(lag_total)
    return (
        inverse.astype(np.float32).astype(jnp.bfloat16),
        forward.astype(np.float32).astype(jnp.bfloat16),
    )


def cos_sin(steps, period):
    quarter = period // 4
    place = steps & (period - 1)
    quadrant = (place + quarter // 2) // quarter
    x = (place - quadrant * quarter).astype(jnp.float32) * (2.0 * math.pi / period)
    y = x * x
    sine = x * (1.0 + y * (-1.0 / 6 + y * (1.0 / 120 - y * (1.0 / 5040))))
    cosine = 1.0 + y * (-0.5 + y * (1.0 / 24 + y * (-1.0 / 720 + y * (1.0 / 40320))))
    odd = (quadrant & 1) == 1
    first = jnp.where(odd, sine, cosine)
    second = jnp.where(odd, cosine, sine)
    first = jnp.where(((quadrant + 1) & 2) == 2, -first, first)
    second = jnp.where((quadrant & 2) == 2, -second, second)
    return first, second


def exchange(source, target, send_sem, recv_sem, day, chan):
    return pltpu.make_async_remote_copy(
        src_ref=source,
        dst_ref=target,
        send_sem=send_sem,
        recv_sem=recv_sem,
        device_id={"days": day, "chan": chan},
        device_id_type=pl.DeviceIdType.MESH,
    )


def pack_halves(spectra_ref, kept, sent, day):
    count, depth, width = spectra_ref.shape
    half = width // 2
    left = lax.broadcasted_iota(jnp.int32, (depth, width), 1) < half
    upper = jnp.full((depth, width), day, jnp.int32) == 1
    for pair in range(count // 2):
        first = spectra_ref[2 * pair].astype(jnp.float32)
        second = spectra_ref[2 * pair + 1].astype(jnp.float32)
        lows = jnp.where(left, first, pltpu.roll(second, half, 1))
        highs = jnp.where(left, pltpu.roll(first, half, 1), second)
        kept[pair] = jnp.where(upper, highs, lows).astype(jnp.bfloat16)
        sent[pair] = jnp.where(upper, lows, highs).astype(jnp.bfloat16)


def source_columns(spectra_ref, sources_ref, chan):
    count, depth, width = spectra_ref.shape
    shape = (count * NSRC, width)
    row = lax.broadcasted_iota(jnp.int32, shape, 0)
    channel = lax.broadcasted_iota(jnp.int32, shape, 1) + chan * width
    wanted = jnp.zeros(shape, jnp.int32)
    for s in range(NSRC):
        wanted = jnp.where(row % NSRC == s, sources_ref[s], wanted)
    total = 0.0
    for w in range(count):
        pick = ((channel == wanted) & (row // NSRC == w)).astype(jnp.float32).astype(jnp.bfloat16)
        total = total + lax.dot_general(
            pick, spectra_ref[w], (((1,), (1,)), ((), ())), preferred_element_type=jnp.float32
        )
    return total.astype(jnp.bfloat16)


def correlate(x_ref, source_rows, inverse_ref, analytic, first_slot, pairs):
    depth, width = x_ref.shape[1:]
    bins, half = depth // 2, width // 2
    wide = NSRC * width
    shape = (source_rows.shape[0], wide)
    rows = lax.broadcasted_iota(jnp.int32, shape, 0)
    lane = lax.broadcasted_iota(jnp.int32, shape, 1)
    for pair in pairs:
        wanted = (2 * pair + lane % width // half) * NSRC + lane // width
        pick = (rows == wanted).astype(jnp.float32).astype(jnp.bfloat16)
        source = lax.dot_general(
            source_rows, pick, (((0,), (0,)), ((), ())), preferred_element_type=jnp.float32
        )
        channel = x_ref[pair].astype(jnp.float32)
        channel = jnp.concatenate([channel] * NSRC, 1)
        real_s, imag_s = source[:bins], source[bins:]
        real_x, imag_x = channel[:bins], channel[bins:]
        real = (real_s * real_x + imag_s * imag_x).astype(jnp.bfloat16)
        imag = (real_s * imag_x - imag_s * real_x).astype(jnp.bfloat16)
        for piece, value in enumerate((real, imag)):
            analytic[first_slot + pair, piece] = jnp.dot(
                inverse_ref[...], value, preferred_element_type=jnp.float32
            )


def stack_sums(analytic, slots, start, block, bins, totals):
    for slot in slots:
        here, there = pl.ds(start, block), pl.ds(bins + start, block)
        cos_re, sin_re = analytic[slot, 0, here], analytic[slot, 0, there]
        cos_im, sin_im = analytic[slot, 1, here], analytic[slot, 1, there]
        corr = [cos_re - sin_im, cos_re + sin_im]
        hilb = [cos_im + sin_re, cos_im - sin_re]
        if start == 0:
            top = lax.broadcasted_iota(jnp.int32, cos_re.shape, 0) == 0
            corr = [jnp.where(top, cos_re, corr[0]), jnp.where(top, sin_re, corr[1])]
            hilb = [jnp.where(top, cos_im, hilb[0]), jnp.where(top, sin_im, hilb[1])]
        for side in range(2):
            linear, phase_re, phase_im = totals[side]
            over = jnp.minimum(lax.rsqrt(corr[side] * corr[side] + hilb[side] * hilb[side]), 2.0)
            totals[side] = (
                linear + corr[side], phase_re + corr[side] * over, phase_im + hilb[side] * over
            )
    return totals


def first_stacks(analytic, slots, held):
    bins = analytic.shape[2] // 2
    for start in range(0, bins, TILE):
        totals = stack_sums(analytic, slots, start, TILE, bins, [(0.0, 0.0, 0.0)] * 2)
        for side in range(2):
            for index, total in enumerate(totals[side]):
                held[index, pl.ds(side * bins + start, TILE)] = total


def last_stacks(analytic, slots, held, weighted, factor, forward_ref):
    bins, width = analytic.shape[2] // 2, analytic.shape[3] // NSRC
    half = width // 2
    near_side = lax.broadcasted_iota(jnp.int32, (TILE, width), 1) < half

    def fold(value):
        parts = []
        for s in range(NSRC):
            part = value[:, s * width : (s + 1) * width]
            parts.append(part + pltpu.roll(part, half, 1))
        return jnp.where(near_side, parts[0], parts[1])

    results = [[], []]
    spectrum = 0.0
    part = bins // 2
    for start in range(0, bins, TILE):
        totals = [
            tuple(held[index, pl.ds(side * bins + start, TILE)] for index in range(3)) for side in range(2)
        ]
        totals = stack_sums(analytic, slots, start, TILE, bins, totals)
        for side in range(2):
            linear, phase_re, phase_im = (fold(total) for total in totals[side])
            results[side].append(linear * (phase_re * phase_re + phase_im * phase_im) * factor)
            if start % (2 * TILE):
                pair = jnp.concatenate(results[side][-2:], 0).astype(jnp.bfloat16)
                weighted[pl.ds(start // part * bins + side * part + start % part - TILE, 2 * TILE)] = pair
        if (start + TILE) % part == 0:
            here = pl.ds(start // part * bins, bins)
            spectrum = spectrum + lax.dot_general(
                weighted[here], forward_ref[here], (((0,), (0,)), ((), ())), preferred_element_type=jnp.float32
            )
    return spectrum


def own_offsets(offset_ref, half, day):
    row = jnp.broadcast_to(offset_ref[...].reshape(1, 2 * half), (TILE, 2 * half))
    lane = lax.broadcasted_iota(jnp.int32, row.shape, 1)
    return jnp.where(lane // half == day, row, pltpu.roll(row, half, 1))


def phase_table(offsets, phases, first, last, half):
    period = 2 * PERIOD
    per = LANES // half
    sub = lax.broadcasted_iota(jnp.int32, (TILE, LANES), 0)
    lane = lax.broadcasted_iota(jnp.int32, (TILE, LANES), 1)
    side = lane // half
    odd = (2 * sub + 1) * offsets

    def group(number, carry):
        base = number * TILE
        jumps_cos, jumps_sin = cos_sin(((base + sub) * per + side) * (offsets * (2 * TILE)), period)
        for member in range(TILE):
            freq = (base + member) * per + side
            cosine, sine = cos_sin(odd * freq, period)
            jump_cos = jnp.broadcast_to(jumps_cos[member : member + 1], (TILE, LANES))
            jump_sin = jnp.broadcast_to(jumps_sin[member : member + 1], (TILE, LANES))
            twice = 2.0 * jump_cos
            now = [cosine, sine]
            before = [cosine * jump_cos + sine * jump_sin, sine * jump_cos - cosine * jump_sin]
            rows = [[], []]
            for step in range(MIRROR // TILE):
                for piece in range(2):
                    rows[piece].append(now[piece])
                    later = twice * now[piece] - before[piece]
                    before[piece], now[piece] = now[piece], later
            for piece in range(2):
                for step in range(0, MIRROR // TILE, 2):
                    tile = jnp.concatenate(rows[piece][step : step + 2], 0).astype(jnp.bfloat16)
                    phases[base + member, pl.ds(piece * MIRROR + step * TILE, 2 * TILE)] = tile
        return carry

    lax.fori_loop(first // TILE, last // TILE, group, 0)


def centre_table(offsets, centre, half, bins):
    block = LANES // (2 * NSRC)
    column = jnp.broadcast_to(offsets[:1].astype(jnp.float32), (LANES, LANES)).T[:half].astype(jnp.int32)
    lane = lax.broadcasted_iota(jnp.int32, (half, LANES), 1)
    freq = lane % block

    def one(number, carry):
        cosine, sine = cos_sin((number * block + freq) * (column * (NSLOW - 1)), 2 * PERIOD)
        centre[number, 0] = cosine
        centre[number, 1] = jnp.where(lane < LANES // 2, -sine, sine)
        return carry

    lax.fori_loop(0, bins // block, one, 0)


def mask_table(masks):
    block = masks.shape[0]
    lane = lax.broadcasted_iota(jnp.int32, masks.shape[1:], 1) % block
    for f in range(block):
        masks[f] = (lane == f).astype(jnp.float32).astype(jnp.bfloat16)


def turned_spectra(result, centre, spectra_out, half):
    block = LANES // (2 * NSRC)
    lane_block = lax.broadcasted_iota(jnp.int32, (half, LANES), 1) // block % NSRC
    for number in range(spectra_out.shape[0]):
        first, at = number // NSRC * LANES, number % NSRC
        part = 0.0
        for s in range(NSRC):
            value = result[s * half : (s + 1) * half, first : first + LANES]
            value = pltpu.roll(value, (s - at) * block % LANES, 1) if s != at else value
            part = value if s == 0 else jnp.where(lane_block == s, value, part)
        turned = part * centre[number, 0] + pltpu.roll(part, LANES // 2, 1) * centre[number, 1]
        spectra_out[number] = turned.astype(jnp.bfloat16)


def spread_blocks(turned, masks, spread, half):
    value = turned[...]
    for f in range(masks.shape[0]):
        for piece in range(0, half, 2 * TILE):
            place = f * half + piece
            spread[place : place + 2 * TILE] = value[piece : piece + 2 * TILE] * masks[f]


def slant(phases, spread, number, first, last, half):
    count = spread.shape[0] // LANES
    left = []
    for index in range(count):
        place = number * count + index
        left.append(
            jnp.concatenate([phases[place, first:last], phases[place, MIRROR + first : MIRROR + last]], 0)
        )
    result = jnp.dot(jnp.concatenate(left, 1), spread[...], preferred_element_type=jnp.float32)
    even, odd = result[: last - first], pltpu.roll(result[last - first :], LANES // 2, 1)
    odd = jnp.where(lax.broadcasted_iota(jnp.int32, odd.shape, 1) < LANES // 2, -odd, odd)
    return even - odd, even + odd


def kernel(
    windows, scaling, days, chans, spectra_hbm, sources_hbm, offset_hbm, inverse_hbm, forward_hbm, out_ref,
    kept, sent, got, column, columns_far, plane, columns_near, analytic, weighted, turned, centre, masks, spread, phases, held,
    spectra_ref, leaving, arriving, owned, landing, inverse_ref, forward_ref,
    sources_ref, offset_ref, table_sem,
    half_sem, far_sem, near_sem, leave_sem, own_sem,
):
    count, depth, width = spectra_ref.shape
    bins, half = depth // 2, width // 2
    far = chans // NEAR
    rows = NSLOW // chans
    day, chan = lax.axis_index("days"), lax.axis_index("chan")
    high, low = chan // NEAR, chan % NEAR
    table_copies = [
        pltpu.make_async_copy(inverse_hbm, inverse_ref, table_sem.at[0]),
        pltpu.make_async_copy(forward_hbm, forward_ref, table_sem.at[1]),
    ]
    near_peers = [
        (dd, dl, (day + dd) % days, (low + dl) % NEAR)
        for dd in range(days)
        for dl in range(NEAR)
        if dd or dl
    ]
    far_peers = [
        (dd, dh, (day + dd) % days, (high + dh) % far)
        for dd in range(days)
        for dh in range(far)
        if dd or dh
    ]
    barrier = pltpu.get_barrier_semaphore()
    greeted = 0
    for dd, dl, to_day, to_low in near_peers:
        pl.semaphore_signal(
            barrier, inc=1, device_id={"days": to_day, "chan": high * NEAR + to_low},
            device_id_type=pl.DeviceIdType.MESH,
        )
        greeted += 1
    for dd, dh, to_day, to_high in far_peers:
        if dh and not dd:
            pl.semaphore_signal(
                barrier, inc=1, device_id={"days": to_day, "chan": to_high * NEAR + low},
                device_id_type=pl.DeviceIdType.MESH,
            )
            greeted += 1
    spectra_copy = pltpu.make_async_copy(spectra_hbm, spectra_ref, table_sem.at[2])
    sources_copy = pltpu.make_async_copy(sources_hbm, sources_ref, table_sem.at[3])
    offset_copy = pltpu.make_async_copy(offset_hbm, offset_ref, table_sem.at[4])
    copies = [sources_copy, spectra_copy, offset_copy]
    for copy in copies + table_copies:
        copy.start()
    for copy in copies:
        copy.wait()
    column[...] = source_columns(spectra_ref, sources_ref, chan)
    pack_halves(spectra_ref, kept, sent, day)
    pl.semaphore_wait(barrier, greeted)

    far_copies = []
    for dd, dh, to_day, to_high in far_peers:
        if dd == 0:
            copy = exchange(
                column, columns_far.at[dh - 1], far_sem.at[0, dh - 1], far_sem.at[1, dh - 1],
                day, to_high * NEAR + low,
            )
            copy.start()
            far_copies.append(copy)
    half_copies = []
    early = depth // 4
    pieces = [(pair, 0, depth) for pair in range(count // 2 - 1)]
    pieces += [(count // 2 - 1, 0, early), (count // 2 - 1, early, depth - early)]
    for index, (pair, first, size) in enumerate(pieces):
        half_copies.append(exchange(
            sent.at[pair, pl.ds(first, size)], got.at[pair, pl.ds(first, size)],
            half_sem.at[0, index], half_sem.at[1, index], (day + 1) % days, chan,
        ))
    for copy in half_copies[:-1]:
        copy.start()
    offsets = own_offsets(offset_ref, half, day)
    blocks = phases.shape[0]
    phase_table(offsets, phases, 0, blocks // 2, half)
    total = column[...].astype(jnp.float32)
    for index, copy in enumerate(far_copies):
        copy.wait_recv()
        total = total + columns_far[index].astype(jnp.float32)
    plane[...] = total.astype(jnp.bfloat16)
    near_copies = []
    for index, (dd, dl, to_day, to_low) in enumerate(near_peers):
        copy = exchange(
            plane, columns_near.at[index], near_sem.at[0, index], near_sem.at[1, index],
            to_day, high * NEAR + to_low,
        )
        copy.start()
        near_copies.append((dd, copy))
    half_copies[-1].start()
    phase_table(offsets, phases, blocks // 2, blocks, half)
    centre_table(offsets, centre, half, bins)
    mask_table(masks)

    def gather(wanted, value):
        for index, (dd, copy) in enumerate(near_copies):
            if dd == wanted:
                copy.wait_recv()
                value = value + columns_near[index].astype(jnp.float32)
        return value.astype(jnp.bfloat16)

    pairs = count // 2
    rows_own = gather(0, total)
    for copy in table_copies:
        copy.wait()
    correlate(kept, rows_own, inverse_ref, analytic, 0, range(pairs))
    first_stacks(analytic, range(pairs), held)
    rows_other = gather(1, 0.0)
    for pair in range(pairs):
        for copy in half_copies[pair : pair + 1 if pair < pairs - 1 else None]:
            copy.wait_recv()
        correlate(got, rows_other, inverse_ref, analytic, pairs, [pair])
    others = range(pairs, 2 * pairs)
    spectrum = last_stacks(analytic, others, held, weighted, scaling / windows**3, forward_ref)
    turned_spectra(spectrum, centre, turned, half)

    wire = leaving.dtype
    blocks_own = turned.shape[0] // days
    leave_copies = []
    edge = max(1, 2 * TILE // (NEAR * rows))
    middle = MIRROR - edge * NEAR * rows

    def work(turn, first, last, spreading):
        target = (day + days - 1 - turn) % days
        for pair in range(blocks_own // 2):
            ends = []
            for at in range(2):
                number = target * blocks_own + 2 * pair + at
                place = spread.at[turn * blocks_own + 2 * pair + at]
                if spreading:
                    spread_blocks(turned.at[number], masks, place, half)
                ends.append(slant(phases, place, number, first, last, half))
            for owner in range(chans):
                upper = owner * rows >= MIRROR
                begin = owner * rows - MIRROR if upper else MIRROR - (owner + 1) * rows
                if first <= begin < last:
                    both = [end[upper][begin - first : begin - first + rows] for end in ends]
                    leaving[target, owner % NEAR, owner // NEAR, pair] = jnp.concatenate(both, 0).astype(wire)

    def leave(turn, cut):
        shift = days - 1 - turn
        target = (day + shift) % days
        at, size = ((0, edge), (far - edge, edge), (edge, far - 2 * edge))[cut]
        for index, (dd, dl, to_day, to_low) in enumerate(near_peers):
            if dd == shift:
                copy = exchange(
                    leaving.at[target, to_low, pl.ds(at, size)], arriving.at[index, pl.ds(at, size)],
                    leave_sem.at[0, cut, index], leave_sem.at[1, cut, index],
                    target, high * NEAR + to_low,
                )
                copy.start()
                leave_copies.append((at, copy))

    for turn in range(days):
        work(turn, middle, MIRROR, True)
        leave(turn, 0)
    for turn in range(days):
        leave(turn, 1)
    for turn in range(days):
        work(turn, 0, middle, False)
        leave(turn, 2)
    for hi in range(far):
        total = leaving[day, low, hi].astype(jnp.float32)
        index = 0
        for at, copy in leave_copies:
            if at == hi:
                copy.wait_recv()
        for index in range(len(near_peers)):
            total = total + arriving[index, hi].astype(jnp.float32)
        owned[hi] = total.astype(wire)
        step = (hi - high) % far
        for dd in range(days):
            def send(dd=dd, hi=hi, step=step):
                exchange(
                    owned.at[hi], landing.at[dd, step], own_sem.at[0, dd, step], own_sem.at[1, dd, step],
                    (day + dd) % days, hi * NEAR + low,
                ).start()

            if dd:
                send()
            else:
                pl.when(step != 0)(send)

    def landed(dd, dh):
        return exchange(
            owned.at[0], landing.at[dd, dh], own_sem.at[0, dd, dh], own_sem.at[1, dd, dh],
            (day + dd) % days, (high + dh) % far * NEAR + low,
        )

    block = LANES // (2 * NSRC)
    for dd in range(days):
        total = 0.0
        for dh in range(far):
            if dd or dh:
                landed(dd, dh).wait_recv()
                total = total + landing[dd, dh].astype(jnp.float32)
            else:
                total = owned[high].astype(jnp.float32)
        pieces = [total[pair, at * rows : (at + 1) * rows] for pair in range(blocks_own // 2) for at in range(2)]
        for part in range(blocks_own * block // LANES):
            some = pieces[part * LANES // block : (part + 1) * LANES // block]
            for s in range(NSRC):
                for p in range(2):
                    begin = (p * NSRC + s) * block
                    value = jnp.concatenate([piece[:, begin : begin + block] for piece in some], 1)
                    mirrored = jnp.concatenate([value[row : row + 1] for row in reversed(range(rows))], 0)
                    lower = jnp.full(value.shape, chan * rows, jnp.int32) < MIRROR
                    out_ref[s, p, (day + dd) % days, part] = jnp.where(lower, mirrored, value)
    for copy in half_copies:
        copy.wait_send()
    for copy in far_copies:
        copy.wait_send()
    for dd, copy in near_copies:
        copy.wait_send()
    for hi, copy in leave_copies:
        copy.wait_send()
    for dd in range(days):
        for dh in range(far):
            if dd or dh:
                landed(dd, dh).wait_send()


def shards(spectra, sources, offsets):
    count, depth, width = spectra.shape
    bins, half = depth // 2, width // 2
    days, chans = lax.axis_size("days"), lax.axis_size("chan")
    windows = count * days
    inverse, forward = tables(bins)
    scaling = windows**1.5 / math.sqrt(width * chans)
    far, rows, pairs = chans // NEAR, NSLOW // chans, count // 2
    near_count = days * NEAR - 1
    wire = jnp.bfloat16 if rows % TILE == 0 else jnp.float32
    block = LANES // (2 * NSRC)
    blocks = bins // block
    chunk = (blocks // days // 2, 2 * rows, LANES)
    parts = bins // days // LANES
    vmem = pl.BlockSpec(memory_space=pltpu.VMEM)
    hbm = pl.BlockSpec(memory_space=pltpu.HBM)
    bf16, f32 = jnp.bfloat16, jnp.float32
    dma = pltpu.SemaphoreType.DMA
    out = pl.pallas_call(
        functools.partial(kernel, windows, scaling, days, chans),
        out_shape=pltpu.VMEM((NSRC, 2, days, parts, rows, LANES), f32),
        in_specs=[hbm] * 5,
        out_specs=vmem,
        scratch_shapes=[
            pltpu.VMEM((pairs, depth, width), bf16),
            pltpu.VMEM((pairs, depth, width), bf16),
            pltpu.VMEM((pairs, depth, width), bf16),
            pltpu.VMEM((count * NSRC, depth), bf16),
            pltpu.VMEM((far - 1, count * NSRC, depth), bf16),
            pltpu.VMEM((count * NSRC, depth), bf16),
            pltpu.VMEM((near_count, count * NSRC, depth), bf16),
            pltpu.VMEM((2 * pairs, 2, depth, NSRC * width), f32),
            pltpu.VMEM((depth, width), bf16),
            pltpu.VMEM((blocks, half, LANES), bf16),
            pltpu.VMEM((blocks, 2, half, LANES), f32),
            pltpu.VMEM((block, 2 * TILE, LANES), bf16),
            pltpu.VMEM((blocks, block * half, LANES), bf16),
            pltpu.VMEM((bins * half // LANES, NSLOW, LANES), bf16),
            pltpu.VMEM((3, depth, NSRC * width), f32),
            pltpu.VMEM((count, depth, width), bf16),
            pltpu.VMEM((days, NEAR, far) + chunk, wire),
            pltpu.VMEM((near_count, far) + chunk, wire),
            pltpu.VMEM((far,) + chunk, wire),
            pltpu.VMEM((days, far) + chunk, wire),
            pltpu.VMEM(inverse.shape, bf16),
            pltpu.VMEM(forward.shape, bf16),
            pltpu.SMEM(sources.shape, jnp.int32),
            pltpu.VMEM(offsets.shape, jnp.int32),
            dma((5,)),
            dma((2, pairs + 1)),
            dma((2, far - 1)),
            dma((2, near_count)),
            dma((2, 3, near_count)),
            dma((2, days, far)),
        ],
        compiler_params=pltpu.CompilerParams(
            collective_id=0, has_side_effects=True, vmem_limit_bytes=56 * 1024 * 1024
        ),
    )(spectra, sources, offsets, jnp.asarray(inverse), jnp.asarray(forward))
    return out.transpose(4, 0, 1, 2, 3, 5).reshape(rows, NSRC, 2, bins)


def solution(mesh):
    placed = (P("days", None, "chan"), P(), P("chan"))
    return jax.shard_map(
        shards, mesh=mesh, in_specs=placed, out_specs=P("chan", None, None, None), check_vma=False
    )
```

```python
import functools
import math

import jax
import jax.numpy as jnp
import numpy as np
from jax import lax
from jax.experimental import pallas as pl
from jax.experimental.pallas import tpu as pltpu
from jax.sharding import PartitionSpec as P

NSLOW = 128
NSRC = 2
PERIOD = 4096
MIRROR = NSLOW // 2
TILE = 8
LANES = 128
NEAR = 4


def tables(bins):
    lag_total = 2 * bins
    lag = np.arange(lag_total)[:, None]
    freq = np.arange(bins)[None, :]
    theta = (lag * freq % lag_total) * (2.0 * math.pi / lag_total)
    cosine, sine = np.cos(theta), np.sin(theta)
    lower = np.concatenate([cosine[bins : bins + 1], sine[1:bins]], 0)
    inverse = np.concatenate([cosine[:bins], lower], 0) / math.sqrt(bins)
    order = np.concatenate([np.arange(bins), [bins], np.arange(lag_total - 1, bins, -1)])
    order = order.reshape(2, 2, -1).transpose(1, 0, 2).reshape(-1)
    cosine, sine = cosine[order], sine[order]
    block = LANES // (2 * NSRC)
    parts = np.stack([cosine, -sine], 1).reshape(lag_total, 2, -1, NSRC, block).transpose(0, 2, 1, 3, 4)
    forward = parts.reshape(lag_total, -1) / math.sqrt(lag_total)
    return (
        inverse.astype(np.float32).astype(jnp.bfloat16),
        forward.astype(np.float32).astype(jnp.bfloat16),
    )


def cos_sin(steps, period):
    quarter = period // 4
    place = steps & (period - 1)
    quadrant = (place + quarter // 2) // quarter
    x = (place - quadrant * quarter).astype(jnp.float32) * (2.0 * math.pi / period)
    y = x * x
    sine = x * (1.0 + y * (-1.0 / 6 + y * (1.0 / 120 - y * (1.0 / 5040))))
    cosine = 1.0 + y * (-0.5 + y * (1.0 / 24 + y * (-1.0 / 720 + y * (1.0 / 40320))))
    odd = (quadrant & 1) == 1
    first = jnp.where(odd, sine, cosine)
    second = jnp.where(odd, cosine, sine)
    first = jnp.where(((quadrant + 1) & 2) == 2, -first, first)
    second = jnp.where((quadrant & 2) == 2, -second, second)
    return first, second


def exchange(source, target, send_sem, recv_sem, day, chan):
    return pltpu.make_async_remote_copy(
        src_ref=source,
        dst_ref=target,
        send_sem=send_sem,
        recv_sem=recv_sem,
        device_id={"days": day, "chan": chan},
        device_id_type=pl.DeviceIdType.MESH,
    )


def pack_halves(spectra_ref, kept, sent, day):
    count, depth, width = spectra_ref.shape
    half = width // 2
    left = lax.broadcasted_iota(jnp.int32, (depth, width), 1) < half
    upper = jnp.full((depth, width), day, jnp.int32) == 1
    for pair in range(count // 2):
        first = spectra_ref[2 * pair].astype(jnp.float32)
        second = spectra_ref[2 * pair + 1].astype(jnp.float32)
        lows = jnp.where(left, first, pltpu.roll(second, half, 1))
        highs = jnp.where(left, pltpu.roll(first, half, 1), second)
        kept[pair] = jnp.where(upper, highs, lows).astype(jnp.bfloat16)
        sent[pair] = jnp.where(upper, lows, highs).astype(jnp.bfloat16)


def source_columns(spectra_ref, sources_ref, chan):
    count, depth, width = spectra_ref.shape
    shape = (count * NSRC, width)
    row = lax.broadcasted_iota(jnp.int32, shape, 0)
    channel = lax.broadcasted_iota(jnp.int32, shape, 1) + chan * width
    wanted = jnp.zeros(shape, jnp.int32)
    for s in range(NSRC):
        wanted = jnp.where(row % NSRC == s, sources_ref[s], wanted)
    total = 0.0
    for w in range(count):
        pick = ((channel == wanted) & (row // NSRC == w)).astype(jnp.float32).astype(jnp.bfloat16)
        total = total + lax.dot_general(
            pick, spectra_ref[w], (((1,), (1,)), ((), ())), preferred_element_type=jnp.float32
        )
    return total.astype(jnp.bfloat16)


def correlate(x_ref, source_rows, inverse_ref, analytic, first_slot, pairs):
    depth, width = x_ref.shape[1:]
    bins, half = depth // 2, width // 2
    wide = NSRC * width
    shape = (source_rows.shape[0], wide)
    rows = lax.broadcasted_iota(jnp.int32, shape, 0)
    lane = lax.broadcasted_iota(jnp.int32, shape, 1)
    for pair in pairs:
        wanted = (2 * pair + lane % width // half) * NSRC + lane // width
        pick = (rows == wanted).astype(jnp.float32).astype(jnp.bfloat16)
        source = lax.dot_general(
            source_rows, pick, (((0,), (0,)), ((), ())), preferred_element_type=jnp.float32
        )
        channel = x_ref[pair].astype(jnp.float32)
        channel = jnp.concatenate([channel] * NSRC, 1)
        real_s, imag_s = source[:bins], source[bins:]
        real_x, imag_x = channel[:bins], channel[bins:]
        real = (real_s * real_x + imag_s * imag_x).astype(jnp.bfloat16)
        imag = (real_s * imag_x - imag_s * real_x).astype(jnp.bfloat16)
        for piece, value in enumerate((real, imag)):
            analytic[first_slot + pair, piece] = jnp.dot(
                inverse_ref[...], value, preferred_element_type=jnp.float32
            )


def stack_sums(analytic, slots, start, block, bins, totals):
    for slot in slots:
        here, there = pl.ds(start, block), pl.ds(bins + start, block)
        cos_re, sin_re = analytic[slot, 0, here], analytic[slot, 0, there]
        cos_im, sin_im = analytic[slot, 1, here], analytic[slot, 1, there]
        corr = [cos_re - sin_im, cos_re + sin_im]
        hilb = [cos_im + sin_re, cos_im - sin_re]
        if start == 0:
            top = lax.broadcasted_iota(jnp.int32, cos_re.shape, 0) == 0
            corr = [jnp.where(top, cos_re, corr[0]), jnp.where(top, sin_re, corr[1])]
            hilb = [jnp.where(top, cos_im, hilb[0]), jnp.where(top, sin_im, hilb[1])]
        for side in range(2):
            linear, phase_re, phase_im = totals[side]
            over = jnp.minimum(lax.rsqrt(corr[side] * corr[side] + hilb[side] * hilb[side]), 2.0)
            totals[side] = (
                linear + corr[side], phase_re + corr[side] * over, phase_im + hilb[side] * over
            )
    return totals


def first_stacks(analytic, slots, held):
    bins = analytic.shape[2] // 2
    for start in range(0, bins, TILE):
        totals = stack_sums(analytic, slots, start, TILE, bins, [(0.0, 0.0, 0.0)] * 2)
        for side in range(2):
            for index, total in enumerate(totals[side]):
                held[index, pl.ds(side * bins + start, TILE)] = total


def last_stacks(analytic, slots, held, weighted, factor, forward_ref):
    bins, width = analytic.shape[2] // 2, analytic.shape[3] // NSRC
    half = width // 2
    near_side = lax.broadcasted_iota(jnp.int32, (TILE, width), 1) < half

    def fold(value):
        parts = []
        for s in range(NSRC):
            part = value[:, s * width : (s + 1) * width]
            parts.append(part + pltpu.roll(part, half, 1))
        return jnp.where(near_side, parts[0], parts[1])

    results = [[], []]
    spectrum = 0.0
    part = bins // 2
    for start in range(0, bins, TILE):
        totals = [
            tuple(held[index, pl.ds(side * bins + start, TILE)] for index in range(3)) for side in range(2)
        ]
        totals = stack_sums(analytic, slots, start, TILE, bins, totals)
        for side in range(2):
            linear, phase_re, phase_im = (fold(total) for total in totals[side])
            results[side].append(linear * (phase_re * phase_re + phase_im * phase_im) * factor)
            if start % (2 * TILE):
                pair = jnp.concatenate(results[side][-2:], 0).astype(jnp.bfloat16)
                weighted[pl.ds(start // part * bins + side * part + start % part - TILE, 2 * TILE)] = pair
        if (start + TILE) % part == 0:
            here = pl.ds(start // part * bins, bins)
            spectrum = spectrum + lax.dot_general(
                weighted[here], forward_ref[here], (((0,), (0,)), ((), ())), preferred_element_type=jnp.float32
            )
    return spectrum


def own_offsets(offset_ref, half, day):
    row = jnp.broadcast_to(offset_ref[...].reshape(1, 2 * half), (TILE, 2 * half))
    lane = lax.broadcasted_iota(jnp.int32, row.shape, 1)
    return jnp.where(lane // half == day, row, pltpu.roll(row, half, 1))


def phase_table(offsets, phases, first, last, half):
    period = 2 * PERIOD
    per = LANES // half
    sub = lax.broadcasted_iota(jnp.int32, (TILE, LANES), 0)
    lane = lax.broadcasted_iota(jnp.int32, (TILE, LANES), 1)
    side = lane // half
    odd = (2 * sub + 1) * offsets

    def group(number, carry):
        base = number * TILE
        jumps_cos, jumps_sin = cos_sin(((base + sub) * per + side) * (offsets * (2 * TILE)), period)
        for member in range(TILE):
            freq = (base + member) * per + side
            cosine, sine = cos_sin(odd * freq, period)
            jump_cos = jnp.broadcast_to(jumps_cos[member : member + 1], (TILE, LANES))
            jump_sin = jnp.broadcast_to(jumps_sin[member : member + 1], (TILE, LANES))
            twice = 2.0 * jump_cos
            now = [cosine, sine]
            before = [cosine * jump_cos + sine * jump_sin, sine * jump_cos - cosine * jump_sin]
            rows = [[], []]
            for step in range(MIRROR // TILE):
                for piece in range(2):
                    rows[piece].append(now[piece])
                    later = twice * now[piece] - before[piece]
                    before[piece], now[piece] = now[piece], later
            for piece in range(2):
                for step in range(0, MIRROR // TILE, 2):
                    tile = jnp.concatenate(rows[piece][step : step + 2], 0).astype(jnp.bfloat16)
                    phases[base + member, pl.ds(piece * MIRROR + step * TILE, 2 * TILE)] = tile
        return carry

    lax.fori_loop(first // TILE, last // TILE, group, 0)


def centre_table(offsets, centre, half, bins):
    block = LANES // (2 * NSRC)
    column = jnp.broadcast_to(offsets[:1].astype(jnp.float32), (LANES, LANES)).T[:half].astype(jnp.int32)
    lane = lax.broadcasted_iota(jnp.int32, (half, LANES), 1)
    freq = lane % block

    def one(number, carry):
        cosine, sine = cos_sin((number * block + freq) * (column * (NSLOW - 1)), 2 * PERIOD)
        centre[number, 0] = cosine
        centre[number, 1] = jnp.where(lane < LANES // 2, -sine, sine)
        return carry

    lax.fori_loop(0, bins // block, one, 0)


def mask_table(masks):
    block = masks.shape[0]
    lane = lax.broadcasted_iota(jnp.int32, masks.shape[1:], 1) % block
    for f in range(block):
        masks[f] = (lane == f).astype(jnp.float32).astype(jnp.bfloat16)


def turned_spectra(result, centre, spectra_out, half):
    block = LANES // (2 * NSRC)
    lane_block = lax.broadcasted_iota(jnp.int32, (half, LANES), 1) // block % NSRC
    for number in range(spectra_out.shape[0]):
        first, at = number // NSRC * LANES, number % NSRC
        part = 0.0
        for s in range(NSRC):
            value = result[s * half : (s + 1) * half, first : first + LANES]
            value = pltpu.roll(value, (s - at) * block % LANES, 1) if s != at else value
            part = value if s == 0 else jnp.where(lane_block == s, value, part)
        turned = part * centre[number, 0] + pltpu.roll(part, LANES // 2, 1) * centre[number, 1]
        spectra_out[number] = turned.astype(jnp.bfloat16)


def slant(phases, turned, masks, number, first, last, half):
    block = masks.shape[0]
    per = LANES // half
    value = turned[number]
    left, right = [], []
    for index in range(block // per):
        place = number * (block // per) + index
        left.append(
            jnp.concatenate([phases[place, first:last], phases[place, MIRROR + first : MIRROR + last]], 0)
        )
        for f in range(index * per, index * per + per):
            right.append(value * jnp.concatenate([masks[f]] * (half // (2 * TILE)), 0))
    result = jnp.dot(jnp.concatenate(left, 1), jnp.concatenate(right, 0), preferred_element_type=jnp.float32)
    even, odd = result[: last - first], pltpu.roll(result[last - first :], LANES // 2, 1)
    odd = jnp.where(lax.broadcasted_iota(jnp.int32, odd.shape, 1) < LANES // 2, -odd, odd)
    return even - odd, even + odd


def kernel(
    windows, scaling, days, chans, spectra_hbm, sources_hbm, offset_hbm, inverse_hbm, forward_hbm, out_ref,
    kept, sent, got, column, columns_far, plane, columns_near, analytic, weighted, turned, centre, masks, phases, held,
    spectra_ref, leaving, arriving, owned, landing, inverse_ref, forward_ref,
    sources_ref, offset_ref, table_sem,
    half_sem, far_sem, near_sem, leave_sem, own_sem,
):
    count, depth, width = spectra_ref.shape
    bins, half = depth // 2, width // 2
    far = chans // NEAR
    rows = NSLOW // chans
    day, chan = lax.axis_index("days"), lax.axis_index("chan")
    high, low = chan // NEAR, chan % NEAR
    table_copies = [
        pltpu.make_async_copy(inverse_hbm, inverse_ref, table_sem.at[0]),
        pltpu.make_async_copy(forward_hbm, forward_ref, table_sem.at[1]),
    ]
    near_peers = [
        (dd, dl, (day + dd) % days, (low + dl) % NEAR)
        for dd in range(days)
        for dl in range(NEAR)
        if dd or dl
    ]
    far_peers = [
        (dd, dh, (day + dd) % days, (high + dh) % far)
        for dd in range(days)
        for dh in range(far)
        if dd or dh
    ]
    barrier = pltpu.get_barrier_semaphore()
    greeted = 0
    for dd, dl, to_day, to_low in near_peers:
        pl.semaphore_signal(
            barrier, inc=1, device_id={"days": to_day, "chan": high * NEAR + to_low},
            device_id_type=pl.DeviceIdType.MESH,
        )
        greeted += 1
    for dd, dh, to_day, to_high in far_peers:
        if dh and not dd:
            pl.semaphore_signal(
                barrier, inc=1, device_id={"days": to_day, "chan": to_high * NEAR + low},
                device_id_type=pl.DeviceIdType.MESH,
            )
            greeted += 1
    spectra_copy = pltpu.make_async_copy(spectra_hbm, spectra_ref, table_sem.at[2])
    sources_copy = pltpu.make_async_copy(sources_hbm, sources_ref, table_sem.at[3])
    offset_copy = pltpu.make_async_copy(offset_hbm, offset_ref, table_sem.at[4])
    copies = [sources_copy, spectra_copy, offset_copy]
    for copy in copies + table_copies:
        copy.start()
    for copy in copies:
        copy.wait()
    column[...] = source_columns(spectra_ref, sources_ref, chan)
    pack_halves(spectra_ref, kept, sent, day)
    pl.semaphore_wait(barrier, greeted)

    far_copies = []
    for dd, dh, to_day, to_high in far_peers:
        if dd == 0:
            copy = exchange(
                column, columns_far.at[dh - 1], far_sem.at[0, dh - 1], far_sem.at[1, dh - 1],
                day, to_high * NEAR + low,
            )
            copy.start()
            far_copies.append(copy)
    half_copies = []
    early = depth // 4
    pieces = [(pair, 0, depth) for pair in range(count // 2 - 1)]
    pieces += [(count // 2 - 1, 0, early), (count // 2 - 1, early, depth - early)]
    for index, (pair, first, size) in enumerate(pieces):
        half_copies.append(exchange(
            sent.at[pair, pl.ds(first, size)], got.at[pair, pl.ds(first, size)],
            half_sem.at[0, index], half_sem.at[1, index], (day + 1) % days, chan,
        ))
    for copy in half_copies[:-1]:
        copy.start()
    offsets = own_offsets(offset_ref, half, day)
    blocks = phases.shape[0]
    phase_table(offsets, phases, 0, blocks // 2, half)
    total = column[...].astype(jnp.float32)
    for index, copy in enumerate(far_copies):
        copy.wait_recv()
        total = total + columns_far[index].astype(jnp.float32)
    plane[...] = total.astype(jnp.bfloat16)
    near_copies = []
    for index, (dd, dl, to_day, to_low) in enumerate(near_peers):
        copy = exchange(
            plane, columns_near.at[index], near_sem.at[0, index], near_sem.at[1, index],
            to_day, high * NEAR + to_low,
        )
        copy.start()
        near_copies.append((dd, copy))
    half_copies[-1].start()
    phase_table(offsets, phases, blocks // 2, blocks, half)
    centre_table(offsets, centre, half, bins)
    mask_table(masks)

    def gather(wanted, value):
        for index, (dd, copy) in enumerate(near_copies):
            if dd == wanted:
                copy.wait_recv()
                value = value + columns_near[index].astype(jnp.float32)
        return value.astype(jnp.bfloat16)

    pairs = count // 2
    rows_own = gather(0, total)
    for copy in table_copies:
        copy.wait()
    correlate(kept, rows_own, inverse_ref, analytic, 0, range(pairs))
    first_stacks(analytic, range(pairs), held)
    rows_other = gather(1, 0.0)
    for pair in range(pairs):
        for copy in half_copies[pair : pair + 1 if pair < pairs - 1 else None]:
            copy.wait_recv()
        correlate(got, rows_other, inverse_ref, analytic, pairs, [pair])
    others = range(pairs, 2 * pairs)
    spectrum = last_stacks(analytic, others, held, weighted, scaling / windows**3, forward_ref)
    turned_spectra(spectrum, centre, turned, half)

    wire = leaving.dtype
    blocks_own = turned.shape[0] // days
    leave_copies = []
    edge = max(1, 2 * TILE // (NEAR * rows))
    middle = MIRROR - edge * NEAR * rows

    def work(turn, first, last):
        target = (day + days - 1 - turn) % days
        for pair in range(blocks_own // 2):
            ends = []
            for at in range(2):
                number = target * blocks_own + 2 * pair + at
                ends.append(slant(phases, turned, masks, number, first, last, half))
            for owner in range(chans):
                upper = owner * rows >= MIRROR
                begin = owner * rows - MIRROR if upper else MIRROR - (owner + 1) * rows
                if first <= begin < last:
                    both = [end[upper][begin - first : begin - first + rows] for end in ends]
                    leaving[target, owner % NEAR, owner // NEAR, pair] = jnp.concatenate(both, 0).astype(wire)

    def leave(turn, cut):
        shift = days - 1 - turn
        target = (day + shift) % days
        at, size = ((0, edge), (edge, far - edge))[cut]
        for index, (dd, dl, to_day, to_low) in enumerate(near_peers):
            if dd == shift:
                copy = exchange(
                    leaving.at[target, to_low, pl.ds(at, size)], arriving.at[index, pl.ds(at, size)],
                    leave_sem.at[0, cut, index], leave_sem.at[1, cut, index],
                    target, high * NEAR + to_low,
                )
                copy.start()
                leave_copies.append((at, copy))

    for turn in range(days):
        work(turn, middle, MIRROR)
        leave(turn, 0)
    for turn in range(days):
        work(turn, 0, middle)
        leave(turn, 1)
    for hi in range(far):
        total = leaving[day, low, hi].astype(jnp.float32)
        index = 0
        for at, copy in leave_copies:
            if at == hi:
                copy.wait_recv()
        for index in range(len(near_peers)):
            total = total + arriving[index, hi].astype(jnp.float32)
        owned[hi] = total.astype(wire)
        step = (hi - high) % far
        for dd in range(days):
            def send(dd=dd, hi=hi, step=step):
                exchange(
                    owned.at[hi], landing.at[dd, step], own_sem.at[0, dd, step], own_sem.at[1, dd, step],
                    (day + dd) % days, hi * NEAR + low,
                ).start()

            if dd:
                send()
            else:
                pl.when(step != 0)(send)

    def landed(dd, dh):
        return exchange(
            owned.at[0], landing.at[dd, dh], own_sem.at[0, dd, dh], own_sem.at[1, dd, dh],
            (day + dd) % days, (high + dh) % far * NEAR + low,
        )

    block = LANES // (2 * NSRC)
    for dd in range(days):
        total = 0.0
        for dh in range(far):
            if dd or dh:
                landed(dd, dh).wait_recv()
                total = total + landing[dd, dh].astype(jnp.float32)
            else:
                total = owned[high].astype(jnp.float32)
        pieces = [total[pair, at * rows : (at + 1) * rows] for pair in range(blocks_own // 2) for at in range(2)]
        for part in range(blocks_own * block // LANES):
            some = pieces[part * LANES // block : (part + 1) * LANES // block]
            for s in range(NSRC):
                for p in range(2):
                    begin = (p * NSRC + s) * block
                    value = jnp.concatenate([piece[:, begin : begin + block] for piece in some], 1)
                    mirrored = jnp.concatenate([value[row : row + 1] for row in reversed(range(rows))], 0)
                    lower = jnp.full(value.shape, chan * rows, jnp.int32) < MIRROR
                    out_ref[s, p, (day + dd) % days, part] = jnp.where(lower, mirrored, value)
    for copy in half_copies:
        copy.wait_send()
    for copy in far_copies:
        copy.wait_send()
    for dd, copy in near_copies:
        copy.wait_send()
    for hi, copy in leave_copies:
        copy.wait_send()
    for dd in range(days):
        for dh in range(far):
            if dd or dh:
                landed(dd, dh).wait_send()


def shards(spectra, sources, offsets):
    count, depth, width = spectra.shape
    bins, half = depth // 2, width // 2
    days, chans = lax.axis_size("days"), lax.axis_size("chan")
    windows = count * days
    inverse, forward = tables(bins)
    scaling = windows**1.5 / math.sqrt(width * chans)
    far, rows, pairs = chans // NEAR, NSLOW // chans, count // 2
    near_count = days * NEAR - 1
    wire = jnp.bfloat16 if rows % TILE == 0 else jnp.float32
    block = LANES // (2 * NSRC)
    blocks = bins // block
    chunk = (blocks // days // 2, 2 * rows, LANES)
    parts = bins // days // LANES
    vmem = pl.BlockSpec(memory_space=pltpu.VMEM)
    hbm = pl.BlockSpec(memory_space=pltpu.HBM)
    bf16, f32 = jnp.bfloat16, jnp.float32
    dma = pltpu.SemaphoreType.DMA
    out = pl.pallas_call(
        functools.partial(kernel, windows, scaling, days, chans),
        out_shape=pltpu.VMEM((NSRC, 2, days, parts, rows, LANES), f32),
        in_specs=[hbm] * 5,
        out_specs=vmem,
        scratch_shapes=[
            pltpu.VMEM((pairs, depth, width), bf16),
            pltpu.VMEM((pairs, depth, width), bf16),
            pltpu.VMEM((pairs, depth, width), bf16),
            pltpu.VMEM((count * NSRC, depth), bf16),
            pltpu.VMEM((far - 1, count * NSRC, depth), bf16),
            pltpu.VMEM((count * NSRC, depth), bf16),
            pltpu.VMEM((near_count, count * NSRC, depth), bf16),
            pltpu.VMEM((2 * pairs, 2, depth, NSRC * width), f32),
            pltpu.VMEM((depth, width), bf16),
            pltpu.VMEM((blocks, half, LANES), bf16),
            pltpu.VMEM((blocks, 2, half, LANES), f32),
            pltpu.VMEM((block, 2 * TILE, LANES), bf16),
            pltpu.VMEM((bins * half // LANES, NSLOW, LANES), bf16),
            pltpu.VMEM((3, depth, NSRC * width), f32),
            pltpu.VMEM((count, depth, width), bf16),
            pltpu.VMEM((days, NEAR, far) + chunk, wire),
            pltpu.VMEM((near_count, far) + chunk, wire),
            pltpu.VMEM((far,) + chunk, wire),
            pltpu.VMEM((days, far) + chunk, wire),
            pltpu.VMEM(inverse.shape, bf16),
            pltpu.VMEM(forward.shape, bf16),
            pltpu.SMEM(sources.shape, jnp.int32),
            pltpu.VMEM(offsets.shape, jnp.int32),
            dma((5,)),
            dma((2, pairs + 1)),
            dma((2, far - 1)),
            dma((2, near_count)),
            dma((2, 2, near_count)),
            dma((2, days, far)),
        ],
        compiler_params=pltpu.CompilerParams(
            collective_id=0, has_side_effects=True, vmem_limit_bytes=56 * 1024 * 1024
        ),
    )(spectra, sources, offsets, jnp.asarray(inverse), jnp.asarray(forward))
    return out.transpose(4, 0, 1, 2, 3, 5).reshape(rows, NSRC, 2, bins)


def solution(mesh):
    placed = (P("days", None, "chan"), P(), P("chan"))
    return jax.shard_map(
        shards, mesh=mesh, in_specs=placed, out_specs=P("chan", None, None, None), check_vma=False
    )
```

```python
import functools
import math

import jax
import jax.numpy as jnp
import numpy as np
from jax import lax
from jax.experimental import pallas as pl
from jax.experimental.pallas import tpu as pltpu
from jax.sharding import PartitionSpec as P

NSLOW = 128
NSRC = 2
PERIOD = 4096
MIRROR = NSLOW // 2
TILE = 8
LANES = 128
NEAR = 4


def tables(bins):
    lag_total = 2 * bins
    lag = np.arange(lag_total)[:, None]
    freq = np.arange(bins)[None, :]
    theta = (lag * freq % lag_total) * (2.0 * math.pi / lag_total)
    cosine, sine = np.cos(theta), np.sin(theta)
    lower = np.concatenate([cosine[bins : bins + 1], sine[1:bins]], 0)
    inverse = np.concatenate([cosine[:bins], lower], 0) / math.sqrt(bins)
    order = np.concatenate([np.arange(bins), [bins], np.arange(lag_total - 1, bins, -1)])
    order = order.reshape(2, 2, -1).transpose(1, 0, 2).reshape(-1)
    cosine, sine = cosine[order], sine[order]
    block = LANES // (2 * NSRC)
    parts = np.stack([cosine, -sine], 1).reshape(lag_total, 2, -1, NSRC, block).transpose(0, 2, 1, 3, 4)
    forward = parts.reshape(lag_total, -1) / math.sqrt(lag_total)
    return (
        inverse.astype(np.float32).astype(jnp.bfloat16),
        forward.astype(np.float32).astype(jnp.bfloat16),
    )


def cos_sin(steps, period):
    quarter = period // 4
    place = steps & (period - 1)
    quadrant = (place + quarter // 2) // quarter
    x = (place - quadrant * quarter).astype(jnp.float32) * (2.0 * math.pi / period)
    y = x * x
    sine = x * (1.0 + y * (-1.0 / 6 + y * (1.0 / 120 - y * (1.0 / 5040))))
    cosine = 1.0 + y * (-0.5 + y * (1.0 / 24 + y * (-1.0 / 720 + y * (1.0 / 40320))))
    odd = (quadrant & 1) == 1
    first = jnp.where(odd, sine, cosine)
    second = jnp.where(odd, cosine, sine)
    first = jnp.where(((quadrant + 1) & 2) == 2, -first, first)
    second = jnp.where((quadrant & 2) == 2, -second, second)
    return first, second


def exchange(source, target, send_sem, recv_sem, day, chan):
    return pltpu.make_async_remote_copy(
        src_ref=source,
        dst_ref=target,
        send_sem=send_sem,
        recv_sem=recv_sem,
        device_id={"days": day, "chan": chan},
        device_id_type=pl.DeviceIdType.MESH,
    )


def pack_halves(spectra_ref, kept, sent, day):
    count, depth, width = spectra_ref.shape
    half = width // 2
    left = lax.broadcasted_iota(jnp.int32, (depth, width), 1) < half
    upper = jnp.full((depth, width), day, jnp.int32) == 1
    for pair in range(count // 2):
        first = spectra_ref[2 * pair].astype(jnp.float32)
        second = spectra_ref[2 * pair + 1].astype(jnp.float32)
        lows = jnp.where(left, first, pltpu.roll(second, half, 1))
        highs = jnp.where(left, pltpu.roll(first, half, 1), second)
        kept[pair] = jnp.where(upper, highs, lows).astype(jnp.bfloat16)
        sent[pair] = jnp.where(upper, lows, highs).astype(jnp.bfloat16)


def source_columns(spectra_ref, sources_ref, chan):
    count, depth, width = spectra_ref.shape
    shape = (count * NSRC, width)
    row = lax.broadcasted_iota(jnp.int32, shape, 0)
    channel = lax.broadcasted_iota(jnp.int32, shape, 1) + chan * width
    wanted = jnp.zeros(shape, jnp.int32)
    for s in range(NSRC):
        wanted = jnp.where(row % NSRC == s, sources_ref[s], wanted)
    total = 0.0
    for w in range(count):
        pick = ((channel == wanted) & (row // NSRC == w)).astype(jnp.float32).astype(jnp.bfloat16)
        total = total + lax.dot_general(
            pick, spectra_ref[w], (((1,), (1,)), ((), ())), preferred_element_type=jnp.float32
        )
    return total.astype(jnp.bfloat16)


def correlate(x_ref, source_rows, inverse_ref, analytic, first_slot, pairs):
    depth, width = x_ref.shape[1:]
    bins, half = depth // 2, width // 2
    wide = NSRC * width
    shape = (source_rows.shape[0], wide)
    rows = lax.broadcasted_iota(jnp.int32, shape, 0)
    lane = lax.broadcasted_iota(jnp.int32, shape, 1)
    for pair in pairs:
        wanted = (2 * pair + lane % width // half) * NSRC + lane // width
        pick = (rows == wanted).astype(jnp.float32).astype(jnp.bfloat16)
        source = lax.dot_general(
            source_rows, pick, (((0,), (0,)), ((), ())), preferred_element_type=jnp.float32
        )
        channel = x_ref[pair].astype(jnp.float32)
        channel = jnp.concatenate([channel] * NSRC, 1)
        real_s, imag_s = source[:bins], source[bins:]
        real_x, imag_x = channel[:bins], channel[bins:]
        real = (real_s * real_x + imag_s * imag_x).astype(jnp.bfloat16)
        imag = (real_s * imag_x - imag_s * real_x).astype(jnp.bfloat16)
        for piece, value in enumerate((real, imag)):
            analytic[first_slot + pair, piece] = jnp.dot(
                inverse_ref[...], value, preferred_element_type=jnp.float32
            )


def stack_sums(analytic, slots, start, block, bins, totals):
    for slot in slots:
        here, there = pl.ds(start, block), pl.ds(bins + start, block)
        cos_re, sin_re = analytic[slot, 0, here], analytic[slot, 0, there]
        cos_im, sin_im = analytic[slot, 1, here], analytic[slot, 1, there]
        corr = [cos_re - sin_im, cos_re + sin_im]
        hilb = [cos_im + sin_re, cos_im - sin_re]
        if start == 0:
            top = lax.broadcasted_iota(jnp.int32, cos_re.shape, 0) == 0
            corr = [jnp.where(top, cos_re, corr[0]), jnp.where(top, sin_re, corr[1])]
            hilb = [jnp.where(top, cos_im, hilb[0]), jnp.where(top, sin_im, hilb[1])]
        for side in range(2):
            linear, phase_re, phase_im = totals[side]
            over = jnp.minimum(lax.rsqrt(corr[side] * corr[side] + hilb[side] * hilb[side]), 2.0)
            totals[side] = (
                linear + corr[side], phase_re + corr[side] * over, phase_im + hilb[side] * over
            )
    return totals


def first_stacks(analytic, slots, held):
    bins = analytic.shape[2] // 2
    for start in range(0, bins, TILE):
        totals = stack_sums(analytic, slots, start, TILE, bins, [(0.0, 0.0, 0.0)] * 2)
        for side in range(2):
            for index, total in enumerate(totals[side]):
                held[index, pl.ds(side * bins + start, TILE)] = total


def last_stacks(analytic, slots, held, weighted, factor, forward_ref):
    bins, width = analytic.shape[2] // 2, analytic.shape[3] // NSRC
    half = width // 2
    near_side = lax.broadcasted_iota(jnp.int32, (TILE, width), 1) < half

    def fold(value):
        parts = []
        for s in range(NSRC):
            part = value[:, s * width : (s + 1) * width]
            parts.append(part + pltpu.roll(part, half, 1))
        return jnp.where(near_side, parts[0], parts[1])

    results = [[], []]
    spectrum = 0.0
    part = bins // 2
    for start in range(0, bins, TILE):
        totals = [
            tuple(held[index, pl.ds(side * bins + start, TILE)] for index in range(3)) for side in range(2)
        ]
        totals = stack_sums(analytic, slots, start, TILE, bins, totals)
        for side in range(2):
            linear, phase_re, phase_im = (fold(total) for total in totals[side])
            results[side].append(linear * (phase_re * phase_re + phase_im * phase_im) * factor)
            if start % (2 * TILE):
                pair = jnp.concatenate(results[side][-2:], 0).astype(jnp.bfloat16)
                weighted[pl.ds(start // part * bins + side * part + start % part - TILE, 2 * TILE)] = pair
        if (start + TILE) % part == 0:
            here = pl.ds(start // part * bins, bins)
            spectrum = spectrum + lax.dot_general(
                weighted[here], forward_ref[here], (((0,), (0,)), ((), ())), preferred_element_type=jnp.float32
            )
    return spectrum


def own_offsets(offset_ref, half, day):
    row = jnp.broadcast_to(offset_ref[...].reshape(1, 2 * half), (TILE, 2 * half))
    lane = lax.broadcasted_iota(jnp.int32, row.shape, 1)
    return jnp.where(lane // half == day, row, pltpu.roll(row, half, 1))


def phase_table(offsets, phases, first, last, half):
    period = 2 * PERIOD
    per = LANES // half
    sub = lax.broadcasted_iota(jnp.int32, (TILE, LANES), 0)
    lane = lax.broadcasted_iota(jnp.int32, (TILE, LANES), 1)
    side = lane // half
    odd = (2 * sub + 1) * offsets

    def group(number, carry):
        base = number * TILE
        jumps_cos, jumps_sin = cos_sin(((base + sub) * per + side) * (offsets * (2 * TILE)), period)
        for member in range(TILE):
            freq = (base + member) * per + side
            cosine, sine = cos_sin(odd * freq, period)
            jump_cos = jnp.broadcast_to(jumps_cos[member : member + 1], (TILE, LANES))
            jump_sin = jnp.broadcast_to(jumps_sin[member : member + 1], (TILE, LANES))
            twice = 2.0 * jump_cos
            now = [cosine, sine]
            before = [cosine * jump_cos + sine * jump_sin, sine * jump_cos - cosine * jump_sin]
            rows = [[], []]
            for step in range(MIRROR // TILE):
                for piece in range(2):
                    rows[piece].append(now[piece])
                    later = twice * now[piece] - before[piece]
                    before[piece], now[piece] = now[piece], later
            for piece in range(2):
                for step in range(0, MIRROR // TILE, 2):
                    tile = jnp.concatenate(rows[piece][step : step + 2], 0).astype(jnp.bfloat16)
                    phases[base + member, pl.ds(piece * MIRROR + step * TILE, 2 * TILE)] = tile
        return carry

    lax.fori_loop(first // TILE, last // TILE, group, 0)


def centre_table(offsets, centre, half, bins):
    block = LANES // (2 * NSRC)
    column = jnp.broadcast_to(offsets[:1].astype(jnp.float32), (LANES, LANES)).T[:half].astype(jnp.int32)
    lane = lax.broadcasted_iota(jnp.int32, (half, LANES), 1)
    freq = lane % block

    def one(number, carry):
        cosine, sine = cos_sin((number * block + freq) * (column * (NSLOW - 1)), 2 * PERIOD)
        centre[number, 0] = cosine
        centre[number, 1] = jnp.where(lane < LANES // 2, -sine, sine)
        return carry

    lax.fori_loop(0, bins // block, one, 0)


def mask_table(masks):
    block = masks.shape[0]
    lane = lax.broadcasted_iota(jnp.int32, masks.shape[1:], 1) % block
    for f in range(block):
        masks[f] = (lane == f).astype(jnp.float32).astype(jnp.bfloat16)


def turned_spectra(result, centre, spectra_out, half):
    block = LANES // (2 * NSRC)
    lane_block = lax.broadcasted_iota(jnp.int32, (half, LANES), 1) // block % NSRC
    for number in range(spectra_out.shape[0]):
        first, at = number // NSRC * LANES, number % NSRC
        part = 0.0
        for s in range(NSRC):
            value = result[s * half : (s + 1) * half, first : first + LANES]
            value = pltpu.roll(value, (s - at) * block % LANES, 1) if s != at else value
            part = value if s == 0 else jnp.where(lane_block == s, value, part)
        turned = part * centre[number, 0] + pltpu.roll(part, LANES // 2, 1) * centre[number, 1]
        spectra_out[number] = turned.astype(jnp.bfloat16)


def slant(phases, turned, masks, number, first, last, half):
    block = masks.shape[0]
    per = LANES // half
    value = turned[number]
    left, right = [], []
    for index in range(block // per):
        place = number * (block // per) + index
        left.append(
            jnp.concatenate([phases[place, first:last], phases[place, MIRROR + first : MIRROR + last]], 0)
        )
        for f in range(index * per, index * per + per):
            right.append(value * jnp.concatenate([masks[f]] * (half // (2 * TILE)), 0))
    result = jnp.dot(jnp.concatenate(left, 1), jnp.concatenate(right, 0), preferred_element_type=jnp.float32)
    even, odd = result[: last - first], pltpu.roll(result[last - first :], LANES // 2, 1)
    odd = jnp.where(lax.broadcasted_iota(jnp.int32, odd.shape, 1) < LANES // 2, -odd, odd)
    return even - odd, even + odd


def kernel(
    windows, scaling, days, chans, spectra_hbm, sources_hbm, offset_hbm, inverse_hbm, forward_hbm, out_ref,
    kept, sent, got, column, columns_far, plane, columns_near, analytic, weighted, turned, centre, masks, phases, held,
    spectra_ref, leaving, arriving, owned, landing, inverse_ref, forward_ref,
    sources_ref, offset_ref, table_sem,
    half_sem, far_sem, near_sem, leave_sem, own_sem,
):
    count, depth, width = spectra_ref.shape
    bins, half = depth // 2, width // 2
    far = chans // NEAR
    rows = NSLOW // chans
    day, chan = lax.axis_index("days"), lax.axis_index("chan")
    high, low = chan // NEAR, chan % NEAR
    table_copies = [
        pltpu.make_async_copy(inverse_hbm, inverse_ref, table_sem.at[0]),
        pltpu.make_async_copy(forward_hbm, forward_ref, table_sem.at[1]),
    ]
    near_peers = [
        (dd, dl, (day + dd) % days, (low + dl) % NEAR)
        for dd in range(days)
        for dl in range(NEAR)
        if dd or dl
    ]
    far_peers = [
        (dd, dh, (day + dd) % days, (high + dh) % far)
        for dd in range(days)
        for dh in range(far)
        if dd or dh
    ]
    barrier = pltpu.get_barrier_semaphore()
    greeted = 0
    for dd, dl, to_day, to_low in near_peers:
        pl.semaphore_signal(
            barrier, inc=1, device_id={"days": to_day, "chan": high * NEAR + to_low},
            device_id_type=pl.DeviceIdType.MESH,
        )
        greeted += 1
    for dd, dh, to_day, to_high in far_peers:
        if dh and not dd:
            pl.semaphore_signal(
                barrier, inc=1, device_id={"days": to_day, "chan": to_high * NEAR + low},
                device_id_type=pl.DeviceIdType.MESH,
            )
            greeted += 1
    spectra_copy = pltpu.make_async_copy(spectra_hbm, spectra_ref, table_sem.at[2])
    sources_copy = pltpu.make_async_copy(sources_hbm, sources_ref, table_sem.at[3])
    offset_copy = pltpu.make_async_copy(offset_hbm, offset_ref, table_sem.at[4])
    copies = [sources_copy, spectra_copy, offset_copy]
    for copy in copies + table_copies:
        copy.start()
    for copy in copies:
        copy.wait()
    column[...] = source_columns(spectra_ref, sources_ref, chan)
    pack_halves(spectra_ref, kept, sent, day)
    pl.semaphore_wait(barrier, greeted)

    far_copies = []
    for dd, dh, to_day, to_high in far_peers:
        if dd == 0:
            copy = exchange(
                column, columns_far.at[dh - 1], far_sem.at[0, dh - 1], far_sem.at[1, dh - 1],
                day, to_high * NEAR + low,
            )
            copy.start()
            far_copies.append(copy)
    half_copies = []
    early = depth * 3 // 8
    pieces = [(pair, 0, depth) for pair in range(count // 2 - 1)]
    pieces += [(count // 2 - 1, 0, early), (count // 2 - 1, early, depth - early)]
    for index, (pair, first, size) in enumerate(pieces):
        half_copies.append(exchange(
            sent.at[pair, pl.ds(first, size)], got.at[pair, pl.ds(first, size)],
            half_sem.at[0, index], half_sem.at[1, index], (day + 1) % days, chan,
        ))
    for copy in half_copies[:-1]:
        copy.start()
    offsets = own_offsets(offset_ref, half, day)
    blocks = phases.shape[0]
    phase_table(offsets, phases, 0, blocks // 2, half)
    total = column[...].astype(jnp.float32)
    for index, copy in enumerate(far_copies):
        copy.wait_recv()
        total = total + columns_far[index].astype(jnp.float32)
    plane[...] = total.astype(jnp.bfloat16)
    near_copies = []
    for index, (dd, dl, to_day, to_low) in enumerate(near_peers):
        copy = exchange(
            plane, columns_near.at[index], near_sem.at[0, index], near_sem.at[1, index],
            to_day, high * NEAR + to_low,
        )
        copy.start()
        near_copies.append((dd, copy))
    half_copies[-1].start()
    phase_table(offsets, phases, blocks // 2, blocks, half)
    centre_table(offsets, centre, half, bins)
    mask_table(masks)

    def gather(wanted, value):
        for index, (dd, copy) in enumerate(near_copies):
            if dd == wanted:
                copy.wait_recv()
                value = value + columns_near[index].astype(jnp.float32)
        return value.astype(jnp.bfloat16)

    pairs = count // 2
    rows_own = gather(0, total)
    for copy in table_copies:
        copy.wait()
    correlate(kept, rows_own, inverse_ref, analytic, 0, range(pairs))
    first_stacks(analytic, range(pairs), held)
    rows_other = gather(1, 0.0)
    for pair in range(pairs):
        for copy in half_copies[pair : pair + 1 if pair < pairs - 1 else None]:
            copy.wait_recv()
        correlate(got, rows_other, inverse_ref, analytic, pairs, [pair])
    others = range(pairs, 2 * pairs)
    spectrum = last_stacks(analytic, others, held, weighted, scaling / windows**3, forward_ref)
    turned_spectra(spectrum, centre, turned, half)

    wire = leaving.dtype
    blocks_own = turned.shape[0] // days
    leave_copies = []
    edge = max(1, 2 * TILE // (NEAR * rows))
    middle = MIRROR - edge * NEAR * rows

    def work(turn, first, last):
        target = (day + days - 1 - turn) % days
        for pair in range(blocks_own // 2):
            ends = []
            for at in range(2):
                number = target * blocks_own + 2 * pair + at
                ends.append(slant(phases, turned, masks, number, first, last, half))
            for owner in range(chans):
                upper = owner * rows >= MIRROR
                begin = owner * rows - MIRROR if upper else MIRROR - (owner + 1) * rows
                if first <= begin < last:
                    both = [end[upper][begin - first : begin - first + rows] for end in ends]
                    leaving[target, owner % NEAR, owner // NEAR, pair] = jnp.concatenate(both, 0).astype(wire)

    def leave(turn, cut):
        shift = days - 1 - turn
        target = (day + shift) % days
        at, size = ((0, edge), (edge, far - edge))[cut]
        for index, (dd, dl, to_day, to_low) in enumerate(near_peers):
            if dd == shift:
                copy = exchange(
                    leaving.at[target, to_low, pl.ds(at, size)], arriving.at[index, pl.ds(at, size)],
                    leave_sem.at[0, cut, index], leave_sem.at[1, cut, index],
                    target, high * NEAR + to_low,
                )
                copy.start()
                leave_copies.append((at, copy))

    for turn in range(days):
        work(turn, middle, MIRROR)
        leave(turn, 0)
    for turn in range(days):
        work(turn, 0, middle)
        leave(turn, 1)
    for hi in range(far):
        total = leaving[day, low, hi].astype(jnp.float32)
        index = 0
        for at, copy in leave_copies:
            if at == hi:
                copy.wait_recv()
        for index in range(len(near_peers)):
            total = total + arriving[index, hi].astype(jnp.float32)
        owned[hi] = total.astype(wire)
        step = (hi - high) % far
        for dd in range(days):
            def send(dd=dd, hi=hi, step=step):
                exchange(
                    owned.at[hi], landing.at[dd, step], own_sem.at[0, dd, step], own_sem.at[1, dd, step],
                    (day + dd) % days, hi * NEAR + low,
                ).start()

            if dd:
                send()
            else:
                pl.when(step != 0)(send)

    def landed(dd, dh):
        return exchange(
            owned.at[0], landing.at[dd, dh], own_sem.at[0, dd, dh], own_sem.at[1, dd, dh],
            (day + dd) % days, (high + dh) % far * NEAR + low,
        )

    block = LANES // (2 * NSRC)
    for dd in range(days):
        total = 0.0
        for dh in range(far):
            if dd or dh:
                landed(dd, dh).wait_recv()
                total = total + landing[dd, dh].astype(jnp.float32)
            else:
                total = owned[high].astype(jnp.float32)
        pieces = [total[pair, at * rows : (at + 1) * rows] for pair in range(blocks_own // 2) for at in range(2)]
        for part in range(blocks_own * block // LANES):
            some = pieces[part * LANES // block : (part + 1) * LANES // block]
            for s in range(NSRC):
                for p in range(2):
                    begin = (p * NSRC + s) * block
                    value = jnp.concatenate([piece[:, begin : begin + block] for piece in some], 1)
                    mirrored = jnp.concatenate([value[row : row + 1] for row in reversed(range(rows))], 0)
                    lower = jnp.full(value.shape, chan * rows, jnp.int32) < MIRROR
                    out_ref[s, p, (day + dd) % days, part] = jnp.where(lower, mirrored, value)
    for copy in half_copies:
        copy.wait_send()
    for copy in far_copies:
        copy.wait_send()
    for dd, copy in near_copies:
        copy.wait_send()
    for hi, copy in leave_copies:
        copy.wait_send()
    for dd in range(days):
        for dh in range(far):
            if dd or dh:
                landed(dd, dh).wait_send()


def shards(spectra, sources, offsets):
    count, depth, width = spectra.shape
    bins, half = depth // 2, width // 2
    days, chans = lax.axis_size("days"), lax.axis_size("chan")
    windows = count * days
    inverse, forward = tables(bins)
    scaling = windows**1.5 / math.sqrt(width * chans)
    far, rows, pairs = chans // NEAR, NSLOW // chans, count // 2
    near_count = days * NEAR - 1
    wire = jnp.bfloat16 if rows % TILE == 0 else jnp.float32
    block = LANES // (2 * NSRC)
    blocks = bins // block
    chunk = (blocks // days // 2, 2 * rows, LANES)
    parts = bins // days // LANES
    vmem = pl.BlockSpec(memory_space=pltpu.VMEM)
    hbm = pl.BlockSpec(memory_space=pltpu.HBM)
    bf16, f32 = jnp.bfloat16, jnp.float32
    dma = pltpu.SemaphoreType.DMA
    out = pl.pallas_call(
        functools.partial(kernel, windows, scaling, days, chans),
        out_shape=pltpu.VMEM((NSRC, 2, days, parts, rows, LANES), f32),
        in_specs=[hbm] * 5,
        out_specs=vmem,
        scratch_shapes=[
            pltpu.VMEM((pairs, depth, width), bf16),
            pltpu.VMEM((pairs, depth, width), bf16),
            pltpu.VMEM((pairs, depth, width), bf16),
            pltpu.VMEM((count * NSRC, depth), bf16),
            pltpu.VMEM((far - 1, count * NSRC, depth), bf16),
            pltpu.VMEM((count * NSRC, depth), bf16),
            pltpu.VMEM((near_count, count * NSRC, depth), bf16),
            pltpu.VMEM((2 * pairs, 2, depth, NSRC * width), f32),
            pltpu.VMEM((depth, width), bf16),
            pltpu.VMEM((blocks, half, LANES), bf16),
            pltpu.VMEM((blocks, 2, half, LANES), f32),
            pltpu.VMEM((block, 2 * TILE, LANES), bf16),
            pltpu.VMEM((bins * half // LANES, NSLOW, LANES), bf16),
            pltpu.VMEM((3, depth, NSRC * width), f32),
            pltpu.VMEM((count, depth, width), bf16),
            pltpu.VMEM((days, NEAR, far) + chunk, wire),
            pltpu.VMEM((near_count, far) + chunk, wire),
            pltpu.VMEM((far,) + chunk, wire),
            pltpu.VMEM((days, far) + chunk, wire),
            pltpu.VMEM(inverse.shape, bf16),
            pltpu.VMEM(forward.shape, bf16),
            pltpu.SMEM(sources.shape, jnp.int32),
            pltpu.VMEM(offsets.shape, jnp.int32),
            dma((5,)),
            dma((2, pairs + 1)),
            dma((2, far - 1)),
            dma((2, near_count)),
            dma((2, 2, near_count)),
            dma((2, days, far)),
        ],
        compiler_params=pltpu.CompilerParams(
            collective_id=0, has_side_effects=True, vmem_limit_bytes=56 * 1024 * 1024
        ),
    )(spectra, sources, offsets, jnp.asarray(inverse), jnp.asarray(forward))
    return out.transpose(4, 0, 1, 2, 3, 5).reshape(rows, NSRC, 2, bins)


def solution(mesh):
    placed = (P("days", None, "chan"), P(), P("chan"))
    return jax.shard_map(
        shards, mesh=mesh, in_specs=placed, out_specs=P("chan", None, None, None), check_vma=False
    )
```

```python
import functools
import math

import jax
import jax.numpy as jnp
import numpy as np
from jax import lax
from jax.experimental import pallas as pl
from jax.experimental.pallas import tpu as pltpu
from jax.sharding import PartitionSpec as P

NSLOW = 128
NSRC = 2
PERIOD = 4096
MIRROR = NSLOW // 2
TILE = 8
LANES = 128
NEAR = 4


def tables(bins):
    lag_total = 2 * bins
    lag = np.arange(lag_total)[:, None]
    freq = np.arange(bins)[None, :]
    theta = (lag * freq % lag_total) * (2.0 * math.pi / lag_total)
    cosine, sine = np.cos(theta), np.sin(theta)
    lower = np.concatenate([cosine[bins : bins + 1], sine[1:bins]], 0)
    inverse = np.concatenate([cosine[:bins], lower], 0) / math.sqrt(bins)
    order = np.concatenate([np.arange(bins), [bins], np.arange(lag_total - 1, bins, -1)])
    order = order.reshape(2, 2, -1).transpose(1, 0, 2).reshape(-1)
    cosine, sine = cosine[order], sine[order]
    block = LANES // (2 * NSRC)
    parts = np.stack([cosine, -sine], 1).reshape(lag_total, 2, -1, NSRC, block).transpose(0, 2, 1, 3, 4)
    forward = parts.reshape(lag_total, -1) / math.sqrt(lag_total)
    return (
        inverse.astype(np.float32).astype(jnp.bfloat16),
        forward.astype(np.float32).astype(jnp.bfloat16),
    )


def cos_sin(steps, period):
    quarter = period // 4
    place = steps & (period - 1)
    quadrant = (place + quarter // 2) // quarter
    x = (place - quadrant * quarter).astype(jnp.float32) * (2.0 * math.pi / period)
    y = x * x
    sine = x * (1.0 + y * (-1.0 / 6 + y * (1.0 / 120 - y * (1.0 / 5040))))
    cosine = 1.0 + y * (-0.5 + y * (1.0 / 24 + y * (-1.0 / 720 + y * (1.0 / 40320))))
    odd = (quadrant & 1) == 1
    first = jnp.where(odd, sine, cosine)
    second = jnp.where(odd, cosine, sine)
    first = jnp.where(((quadrant + 1) & 2) == 2, -first, first)
    second = jnp.where((quadrant & 2) == 2, -second, second)
    return first, second


def exchange(source, target, send_sem, recv_sem, day, chan):
    return pltpu.make_async_remote_copy(
        src_ref=source,
        dst_ref=target,
        send_sem=send_sem,
        recv_sem=recv_sem,
        device_id={"days": day, "chan": chan},
        device_id_type=pl.DeviceIdType.MESH,
    )


def pack_halves(spectra_ref, kept, sent, day):
    count, depth, width = spectra_ref.shape
    half = width // 2
    left = lax.broadcasted_iota(jnp.int32, (depth, width), 1) < half
    upper = jnp.full((depth, width), day, jnp.int32) == 1
    for pair in range(count // 2):
        first = spectra_ref[2 * pair].astype(jnp.float32)
        second = spectra_ref[2 * pair + 1].astype(jnp.float32)
        lows = jnp.where(left, first, pltpu.roll(second, half, 1))
        highs = jnp.where(left, pltpu.roll(first, half, 1), second)
        kept[pair] = jnp.where(upper, highs, lows).astype(jnp.bfloat16)
        sent[pair] = jnp.where(upper, lows, highs).astype(jnp.bfloat16)


def source_columns(spectra_ref, sources_ref, chan):
    count, depth, width = spectra_ref.shape
    shape = (count * NSRC, width)
    row = lax.broadcasted_iota(jnp.int32, shape, 0)
    channel = lax.broadcasted_iota(jnp.int32, shape, 1) + chan * width
    wanted = jnp.zeros(shape, jnp.int32)
    for s in range(NSRC):
        wanted = jnp.where(row % NSRC == s, sources_ref[s], wanted)
    total = 0.0
    for w in range(count):
        pick = ((channel == wanted) & (row // NSRC == w)).astype(jnp.float32).astype(jnp.bfloat16)
        total = total + lax.dot_general(
            pick, spectra_ref[w], (((1,), (1,)), ((), ())), preferred_element_type=jnp.float32
        )
    return total.astype(jnp.bfloat16)


def correlate(x_ref, source_rows, inverse_ref, analytic, first_slot, pairs):
    depth, width = x_ref.shape[1:]
    bins, half = depth // 2, width // 2
    wide = NSRC * width
    shape = (source_rows.shape[0], wide)
    rows = lax.broadcasted_iota(jnp.int32, shape, 0)
    lane = lax.broadcasted_iota(jnp.int32, shape, 1)
    for pair in pairs:
        wanted = (2 * pair + lane % width // half) * NSRC + lane // width
        pick = (rows == wanted).astype(jnp.float32).astype(jnp.bfloat16)
        source = lax.dot_general(
            source_rows, pick, (((0,), (0,)), ((), ())), preferred_element_type=jnp.float32
        )
        channel = x_ref[pair].astype(jnp.float32)
        channel = jnp.concatenate([channel] * NSRC, 1)
        real_s, imag_s = source[:bins], source[bins:]
        real_x, imag_x = channel[:bins], channel[bins:]
        real = (real_s * real_x + imag_s * imag_x).astype(jnp.bfloat16)
        imag = (real_s * imag_x - imag_s * real_x).astype(jnp.bfloat16)
        for piece, value in enumerate((real, imag)):
            analytic[first_slot + pair, piece] = jnp.dot(
                inverse_ref[...], value, preferred_element_type=jnp.float32
            )


def stack_sums(analytic, slots, start, block, bins, totals):
    for slot in slots:
        here, there = pl.ds(start, block), pl.ds(bins + start, block)
        cos_re, sin_re = analytic[slot, 0, here], analytic[slot, 0, there]
        cos_im, sin_im = analytic[slot, 1, here], analytic[slot, 1, there]
        corr = [cos_re - sin_im, cos_re + sin_im]
        hilb = [cos_im + sin_re, cos_im - sin_re]
        if start == 0:
            top = lax.broadcasted_iota(jnp.int32, cos_re.shape, 0) == 0
            corr = [jnp.where(top, cos_re, corr[0]), jnp.where(top, sin_re, corr[1])]
            hilb = [jnp.where(top, cos_im, hilb[0]), jnp.where(top, sin_im, hilb[1])]
        for side in range(2):
            linear, phase_re, phase_im = totals[side]
            over = jnp.minimum(lax.rsqrt(corr[side] * corr[side] + hilb[side] * hilb[side]), 2.0)
            totals[side] = (
                linear + corr[side], phase_re + corr[side] * over, phase_im + hilb[side] * over
            )
    return totals


def first_stacks(analytic, slots, held):
    bins = analytic.shape[2] // 2
    for start in range(0, bins, TILE):
        totals = stack_sums(analytic, slots, start, TILE, bins, [(0.0, 0.0, 0.0)] * 2)
        for side in range(2):
            for index, total in enumerate(totals[side]):
                held[index, pl.ds(side * bins + start, TILE)] = total


def last_stacks(analytic, slots, held, weighted, factor, forward_ref):
    bins, width = analytic.shape[2] // 2, analytic.shape[3] // NSRC
    half = width // 2
    near_side = lax.broadcasted_iota(jnp.int32, (TILE, width), 1) < half

    def fold(value):
        parts = []
        for s in range(NSRC):
            part = value[:, s * width : (s + 1) * width]
            parts.append(part + pltpu.roll(part, half, 1))
        return jnp.where(near_side, parts[0], parts[1])

    results = [[], []]
    spectrum = 0.0
    part = bins // 2
    for start in range(0, bins, TILE):
        totals = [
            tuple(held[index, pl.ds(side * bins + start, TILE)] for index in range(3)) for side in range(2)
        ]
        totals = stack_sums(analytic, slots, start, TILE, bins, totals)
        for side in range(2):
            linear, phase_re, phase_im = (fold(total) for total in totals[side])
            results[side].append(linear * (phase_re * phase_re + phase_im * phase_im) * factor)
            if start % (2 * TILE):
                pair = jnp.concatenate(results[side][-2:], 0).astype(jnp.bfloat16)
                weighted[pl.ds(start // part * bins + side * part + start % part - TILE, 2 * TILE)] = pair
        if (start + TILE) % part == 0:
            here = pl.ds(start // part * bins, bins)
            spectrum = spectrum + lax.dot_general(
                weighted[here], forward_ref[here], (((0,), (0,)), ((), ())), preferred_element_type=jnp.float32
            )
    return spectrum


def own_offsets(offset_ref, half, day):
    row = jnp.broadcast_to(offset_ref[...].reshape(1, 2 * half), (TILE, 2 * half))
    lane = lax.broadcasted_iota(jnp.int32, row.shape, 1)
    return jnp.where(lane // half == day, row, pltpu.roll(row, half, 1))


def phase_table(offsets, phases, first, last, half):
    period = 2 * PERIOD
    per = LANES // half
    sub = lax.broadcasted_iota(jnp.int32, (TILE, LANES), 0)
    lane = lax.broadcasted_iota(jnp.int32, (TILE, LANES), 1)
    side = lane // half
    odd = (2 * sub + 1) * offsets

    def group(number, carry):
        base = number * TILE
        jumps_cos, jumps_sin = cos_sin(((base + sub) * per + side) * (offsets * (2 * TILE)), period)
        for member in range(TILE):
            freq = (base + member) * per + side
            cosine, sine = cos_sin(odd * freq, period)
            jump_cos = jnp.broadcast_to(jumps_cos[member : member + 1], (TILE, LANES))
            jump_sin = jnp.broadcast_to(jumps_sin[member : member + 1], (TILE, LANES))
            twice = 2.0 * jump_cos
            now = [cosine, sine]
            before = [cosine * jump_cos + sine * jump_sin, sine * jump_cos - cosine * jump_sin]
            rows = [[], []]
            for step in range(MIRROR // TILE):
                for piece in range(2):
                    rows[piece].append(now[piece])
                    later = twice * now[piece] - before[piece]
                    before[piece], now[piece] = now[piece], later
            for piece in range(2):
                for step in range(0, MIRROR // TILE, 2):
                    tile = jnp.concatenate(rows[piece][step : step + 2], 0).astype(jnp.bfloat16)
                    phases[base + member, pl.ds(piece * MIRROR + step * TILE, 2 * TILE)] = tile
        return carry

    lax.fori_loop(first // TILE, last // TILE, group, 0)


def centre_table(offsets, centre, half, bins):
    block = LANES // (2 * NSRC)
    column = jnp.broadcast_to(offsets[:1].astype(jnp.float32), (LANES, LANES)).T[:half].astype(jnp.int32)
    lane = lax.broadcasted_iota(jnp.int32, (half, LANES), 1)
    freq = lane % block

    def one(number, carry):
        cosine, sine = cos_sin((number * block + freq) * (column * (NSLOW - 1)), 2 * PERIOD)
        centre[number, 0] = cosine
        centre[number, 1] = jnp.where(lane < LANES // 2, -sine, sine)
        return carry

    lax.fori_loop(0, bins // block, one, 0)


def mask_table(masks):
    block = masks.shape[0]
    lane = lax.broadcasted_iota(jnp.int32, masks.shape[1:], 1) % block
    for f in range(block):
        masks[f] = (lane == f).astype(jnp.float32).astype(jnp.bfloat16)


def turned_spectra(result, centre, spectra_out, half):
    block = LANES // (2 * NSRC)
    lane_block = lax.broadcasted_iota(jnp.int32, (half, LANES), 1) // block % NSRC
    for number in range(spectra_out.shape[0]):
        first, at = number // NSRC * LANES, number % NSRC
        part = 0.0
        for s in range(NSRC):
            value = result[s * half : (s + 1) * half, first : first + LANES]
            value = pltpu.roll(value, (s - at) * block % LANES, 1) if s != at else value
            part = value if s == 0 else jnp.where(lane_block == s, value, part)
        turned = part * centre[number, 0] + pltpu.roll(part, LANES // 2, 1) * centre[number, 1]
        spectra_out[number] = turned.astype(jnp.bfloat16)


def slant(phases, turned, masks, number, first, last, half):
    block = masks.shape[0]
    per = LANES // half
    value = turned[number]
    left, right = [], []
    for index in range(block // per):
        place = number * (block // per) + index
        left.append(
            jnp.concatenate([phases[place, first:last], phases[place, MIRROR + first : MIRROR + last]], 0)
        )
        for f in range(index * per, index * per + per):
            right.append(value * jnp.concatenate([masks[f]] * (half // (2 * TILE)), 0))
    result = jnp.dot(jnp.concatenate(left, 1), jnp.concatenate(right, 0), preferred_element_type=jnp.float32)
    even, odd = result[: last - first], pltpu.roll(result[last - first :], LANES // 2, 1)
    odd = jnp.where(lax.broadcasted_iota(jnp.int32, odd.shape, 1) < LANES // 2, -odd, odd)
    return even - odd, even + odd


def kernel(
    windows, scaling, days, chans, spectra_hbm, sources_hbm, offset_hbm, inverse_hbm, forward_hbm, out_ref,
    kept, sent, got, column, columns_far, plane, columns_near, analytic, weighted, turned, centre, masks, phases, held,
    spectra_ref, leaving, arriving, owned, landing, inverse_ref, forward_ref,
    sources_ref, offset_ref, table_sem,
    half_sem, far_sem, near_sem, leave_sem, own_sem,
):
    count, depth, width = spectra_ref.shape
    bins, half = depth // 2, width // 2
    far = chans // NEAR
    rows = NSLOW // chans
    day, chan = lax.axis_index("days"), lax.axis_index("chan")
    high, low = chan // NEAR, chan % NEAR
    table_copies = [
        pltpu.make_async_copy(inverse_hbm, inverse_ref, table_sem.at[0]),
        pltpu.make_async_copy(forward_hbm, forward_ref, table_sem.at[1]),
    ]
    near_peers = [
        (dd, dl, (day + dd) % days, (low + dl) % NEAR)
        for dd in reversed(range(days))
        for dl in range(NEAR)
        if dd or dl
    ]
    far_peers = [
        (dd, dh, (day + dd) % days, (high + dh) % far)
        for dd in range(days)
        for dh in range(far)
        if dd or dh
    ]
    barrier = pltpu.get_barrier_semaphore()
    greeted = 0
    for dd, dl, to_day, to_low in near_peers:
        pl.semaphore_signal(
            barrier, inc=1, device_id={"days": to_day, "chan": high * NEAR + to_low},
            device_id_type=pl.DeviceIdType.MESH,
        )
        greeted += 1
    for dd, dh, to_day, to_high in far_peers:
        if dh and not dd:
            pl.semaphore_signal(
                barrier, inc=1, device_id={"days": to_day, "chan": to_high * NEAR + low},
                device_id_type=pl.DeviceIdType.MESH,
            )
            greeted += 1
    spectra_copy = pltpu.make_async_copy(spectra_hbm, spectra_ref, table_sem.at[2])
    sources_copy = pltpu.make_async_copy(sources_hbm, sources_ref, table_sem.at[3])
    offset_copy = pltpu.make_async_copy(offset_hbm, offset_ref, table_sem.at[4])
    copies = [sources_copy, spectra_copy, offset_copy]
    for copy in copies + table_copies:
        copy.start()
    for copy in copies:
        copy.wait()
    column[...] = source_columns(spectra_ref, sources_ref, chan)
    pack_halves(spectra_ref, kept, sent, day)
    pl.semaphore_wait(barrier, greeted)

    far_copies = []
    for dd, dh, to_day, to_high in far_peers:
        if dd == 0:
            copy = exchange(
                column, columns_far.at[dh - 1], far_sem.at[0, dh - 1], far_sem.at[1, dh - 1],
                day, to_high * NEAR + low,
            )
            copy.start()
            far_copies.append(copy)
    half_copies = []
    early = depth * 7 // 16
    pieces = [(pair, 0, depth) for pair in range(count // 2 - 1)]
    pieces += [(count // 2 - 1, 0, early), (count // 2 - 1, early, depth - early)]
    for index, (pair, first, size) in enumerate(pieces):
        half_copies.append(exchange(
            sent.at[pair, pl.ds(first, size)], got.at[pair, pl.ds(first, size)],
            half_sem.at[0, index], half_sem.at[1, index], (day + 1) % days, chan,
        ))
    for copy in half_copies[:-1]:
        copy.start()
    offsets = own_offsets(offset_ref, half, day)
    blocks = phases.shape[0]
    phase_table(offsets, phases, 0, blocks // 2, half)
    total = column[...].astype(jnp.float32)
    for index, copy in enumerate(far_copies):
        copy.wait_recv()
        total = total + columns_far[index].astype(jnp.float32)
    plane[...] = total.astype(jnp.bfloat16)
    near_copies = []
    for index, (dd, dl, to_day, to_low) in enumerate(near_peers):
        copy = exchange(
            plane, columns_near.at[index], near_sem.at[0, index], near_sem.at[1, index],
            to_day, high * NEAR + to_low,
        )
        copy.start()
        near_copies.append((dd, copy))
    half_copies[-1].start()
    phase_table(offsets, phases, blocks // 2, blocks, half)
    centre_table(offsets, centre, half, bins)
    mask_table(masks)

    def gather(wanted, value):
        for index, (dd, copy) in enumerate(near_copies):
            if dd == wanted:
                copy.wait_recv()
                value = value + columns_near[index].astype(jnp.float32)
        return value.astype(jnp.bfloat16)

    pairs = count // 2
    rows_own = gather(0, total)
    for copy in table_copies:
        copy.wait()
    correlate(kept, rows_own, inverse_ref, analytic, 0, range(pairs))
    first_stacks(analytic, range(pairs), held)
    rows_other = gather(1, 0.0)
    for pair in range(pairs):
        for copy in half_copies[pair : pair + 1 if pair < pairs - 1 else None]:
            copy.wait_recv()
        correlate(got, rows_other, inverse_ref, analytic, pairs, [pair])
    others = range(pairs, 2 * pairs)
    spectrum = last_stacks(analytic, others, held, weighted, scaling / windows**3, forward_ref)
    turned_spectra(spectrum, centre, turned, half)

    wire = leaving.dtype
    blocks_own = turned.shape[0] // days
    leave_copies = []
    edge = max(1, 2 * TILE // (NEAR * rows))
    middle = MIRROR - edge * NEAR * rows

    def work(turn, first, last):
        target = (day + days - 1 - turn) % days
        for pair in range(blocks_own // 2):
            ends = []
            for at in range(2):
                number = target * blocks_own + 2 * pair + at
                ends.append(slant(phases, turned, masks, number, first, last, half))
            for owner in range(chans):
                upper = owner * rows >= MIRROR
                begin = owner * rows - MIRROR if upper else MIRROR - (owner + 1) * rows
                if first <= begin < last:
                    both = [end[upper][begin - first : begin - first + rows] for end in ends]
                    leaving[target, owner % NEAR, owner // NEAR, pair] = jnp.concatenate(both, 0).astype(wire)

    def leave(turn, cut):
        shift = days - 1 - turn
        target = (day + shift) % days
        at, size = ((0, edge), (edge, far - edge))[cut]
        for index, (dd, dl, to_day, to_low) in enumerate(near_peers):
            if dd == shift:
                copy = exchange(
                    leaving.at[target, to_low, pl.ds(at, size)], arriving.at[index, pl.ds(at, size)],
                    leave_sem.at[0, cut, index], leave_sem.at[1, cut, index],
                    target, high * NEAR + to_low,
                )
                copy.start()
                leave_copies.append((at, copy))

    for turn in range(days):
        work(turn, middle, MIRROR)
        leave(turn, 0)
    for turn in range(days):
        work(turn, 0, middle)
        leave(turn, 1)
    for hi in range(far):
        total = leaving[day, low, hi].astype(jnp.float32)
        index = 0
        for at, copy in leave_copies:
            if at == hi:
                copy.wait_recv()
        for index in range(len(near_peers)):
            total = total + arriving[index, hi].astype(jnp.float32)
        owned[hi] = total.astype(wire)
        step = (hi - high) % far
        for dd in range(days):
            def send(dd=dd, hi=hi, step=step):
                exchange(
                    owned.at[hi], landing.at[dd, step], own_sem.at[0, dd, step], own_sem.at[1, dd, step],
                    (day + dd) % days, hi * NEAR + low,
                ).start()

            if dd:
                send()
            else:
                pl.when(step != 0)(send)

    def landed(dd, dh):
        return exchange(
            owned.at[0], landing.at[dd, dh], own_sem.at[0, dd, dh], own_sem.at[1, dd, dh],
            (day + dd) % days, (high + dh) % far * NEAR + low,
        )

    block = LANES // (2 * NSRC)
    for dd in range(days):
        total = 0.0
        for dh in range(far):
            if dd or dh:
                landed(dd, dh).wait_recv()
                total = total + landing[dd, dh].astype(jnp.float32)
            else:
                total = owned[high].astype(jnp.float32)
        pieces = [total[pair, at * rows : (at + 1) * rows] for pair in range(blocks_own // 2) for at in range(2)]
        for part in range(blocks_own * block // LANES):
            some = pieces[part * LANES // block : (part + 1) * LANES // block]
            for s in range(NSRC):
                for p in range(2):
                    begin = (p * NSRC + s) * block
                    value = jnp.concatenate([piece[:, begin : begin + block] for piece in some], 1)
                    mirrored = jnp.concatenate([value[row : row + 1] for row in reversed(range(rows))], 0)
                    lower = jnp.full(value.shape, chan * rows, jnp.int32) < MIRROR
                    out_ref[s, p, (day + dd) % days, part] = jnp.where(lower, mirrored, value)
    for copy in half_copies:
        copy.wait_send()
    for copy in far_copies:
        copy.wait_send()
    for dd, copy in near_copies:
        copy.wait_send()
    for hi, copy in leave_copies:
        copy.wait_send()
    for dd in range(days):
        for dh in range(far):
            if dd or dh:
                landed(dd, dh).wait_send()


def shards(spectra, sources, offsets):
    count, depth, width = spectra.shape
    bins, half = depth // 2, width // 2
    days, chans = lax.axis_size("days"), lax.axis_size("chan")
    windows = count * days
    inverse, forward = tables(bins)
    scaling = windows**1.5 / math.sqrt(width * chans)
    far, rows, pairs = chans // NEAR, NSLOW // chans, count // 2
    near_count = days * NEAR - 1
    wire = jnp.bfloat16 if rows % TILE == 0 else jnp.float32
    block = LANES // (2 * NSRC)
    blocks = bins // block
    chunk = (blocks // days // 2, 2 * rows, LANES)
    parts = bins // days // LANES
    vmem = pl.BlockSpec(memory_space=pltpu.VMEM)
    hbm = pl.BlockSpec(memory_space=pltpu.HBM)
    bf16, f32 = jnp.bfloat16, jnp.float32
    dma = pltpu.SemaphoreType.DMA
    out = pl.pallas_call(
        functools.partial(kernel, windows, scaling, days, chans),
        out_shape=pltpu.VMEM((NSRC, 2, days, parts, rows, LANES), f32),
        in_specs=[hbm] * 5,
        out_specs=vmem,
        scratch_shapes=[
            pltpu.VMEM((pairs, depth, width), bf16),
            pltpu.VMEM((pairs, depth, width), bf16),
            pltpu.VMEM((pairs, depth, width), bf16),
            pltpu.VMEM((count * NSRC, depth), bf16),
            pltpu.VMEM((far - 1, count * NSRC, depth), bf16),
            pltpu.VMEM((count * NSRC, depth), bf16),
            pltpu.VMEM((near_count, count * NSRC, depth), bf16),
            pltpu.VMEM((2 * pairs, 2, depth, NSRC * width), f32),
            pltpu.VMEM((depth, width), bf16),
            pltpu.VMEM((blocks, half, LANES), bf16),
            pltpu.VMEM((blocks, 2, half, LANES), f32),
            pltpu.VMEM((block, 2 * TILE, LANES), bf16),
            pltpu.VMEM((bins * half // LANES, NSLOW, LANES), bf16),
            pltpu.VMEM((3, depth, NSRC * width), f32),
            pltpu.VMEM((count, depth, width), bf16),
            pltpu.VMEM((days, NEAR, far) + chunk, wire),
            pltpu.VMEM((near_count, far) + chunk, wire),
            pltpu.VMEM((far,) + chunk, wire),
            pltpu.VMEM((days, far) + chunk, wire),
            pltpu.VMEM(inverse.shape, bf16),
            pltpu.VMEM(forward.shape, bf16),
            pltpu.SMEM(sources.shape, jnp.int32),
            pltpu.VMEM(offsets.shape, jnp.int32),
            dma((5,)),
            dma((2, pairs + 1)),
            dma((2, far - 1)),
            dma((2, near_count)),
            dma((2, 2, near_count)),
            dma((2, days, far)),
        ],
        compiler_params=pltpu.CompilerParams(
            collective_id=0, has_side_effects=True, vmem_limit_bytes=56 * 1024 * 1024
        ),
    )(spectra, sources, offsets, jnp.asarray(inverse), jnp.asarray(forward))
    return out.transpose(4, 0, 1, 2, 3, 5).reshape(rows, NSRC, 2, bins)


def solution(mesh):
    placed = (P("days", None, "chan"), P(), P("chan"))
    return jax.shard_map(
        shards, mesh=mesh, in_specs=placed, out_specs=P("chan", None, None, None), check_vma=False
    )
```
